128 devices in a mesh: emb: 4 (over x), row: 16 (over z, y), phase: 2 (over core).
Axes of the slice: x: 4, y: 4, z: 4, core: 2. Of those that a mesh axis runs over, the one named last changes fastest.
Arguments:
- item_table: bfloat16 [4096, 512], P('emb'), may hold values from -10 to 10
- item_owner: int32 [4, 2, 4096, 1], P('emb', 'phase', 'row'), may hold values from 0 to 3; in each aligned block of 256 rows (0 to 255, 256 to 511, ..., all dimensions but the last counted through in order) at most 128 rows name the same one
- item_slot: int32 [4, 2, 4096], P('emb', 'phase', 'row'), may hold values from 0 to 1023
- seq_lengths: int32 [4, 2, 2], P('emb'), may hold values from 1 to 3072, 4096 in all within a row
- row_grads: bfloat16 [4, 2, 4096, 512], P('emb', 'phase', 'row'), may hold values from -6 to 6
- proj_weight: bfloat16 [2, 512, 2048], P('phase'), may hold values from -2 to 2
- out_weight: bfloat16 [2, 512, 512], P('phase'), may hold values from -0.25 to 0.25
- final_gain: float32 [512], replicated, may hold values from 0.1 to 1.9
Outputs:
- sequence_states: bfloat16 [4, 2, 4096, 512], P('emb', 'phase', 'row')
- table_grad: float32 [4096, 512], P(('emb', 'row', 'phase'))
The draws below stay inside these ranges and needn't reach their ends.
Inputs may be any that keep to these rules, and one draw needn't show every extreme that they name: `item_owner`: among the 256 tokens of one device, at most 128 name the same owner, and in every draw some device has an owner named by exactly 128 of its tokens. `seq_lengths`: the 2 lengths of one micro-batch of one group sum to 4096; neither is longer than 3072.
All inputs are finite; a program needn't handle non-finite values.
Results may differ from the reference program's by a relative error of at most 0.013.
Values may be sent and summed in bfloat16 or wider, within the bound.
A program may use at most 64 MiB of HBM per device.

```python
import math
import jax
import jax.numpy as jnp
import numpy as np
from jax import lax

D = 512
HEADS = 4
HEAD_DIM = 128
V_DEV = 1024
TOK_DEV = 256
MICRO = 2
SEQS = 2
GROUP_TOK = 4096
MAXLEN = 3072
CAP = 128
VOCAB = 4096
N_EMB = 4
N_PHASE = 2


def common_direction(key):
    raw_vector = jax.random.truncated_normal(jax.random.fold_in(key, 7), -4.0, 4.0, (D,), jnp.float32)
    return raw_vector / jnp.sqrt(jnp.sum(raw_vector * raw_vector))


def draw_item_table(key, part):
    direction = common_direction(key)
    noise_rows = jax.random.truncated_normal(jax.random.fold_in(key, 11), -4.0, 4.0, (VOCAB, D), jnp.float32)
    table_rows = math.sqrt(D) * direction[None, :] + noise_rows
    return jnp.clip(table_rows, -10.0, 10.0).astype(jnp.bfloat16)


def draw_proj_weight(key, part):
    direction = common_direction(key)
    columns = 4 * HEADS * HEAD_DIM
    inner_width = HEADS * HEAD_DIM
    base_draw = jax.random.truncated_normal(jax.random.fold_in(key, 13), -4.0, 4.0, (N_PHASE, D, columns), jnp.float32)
    along_dir = jnp.einsum('d,sdc->sc', direction, base_draw)
    base_perp = base_draw - direction[None, :, None] * along_dir[:, None, :]
    unit_scale = math.sqrt(2.0 / D)
    is_gate = jnp.arange(columns) < inner_width
    column_scale = jnp.where(is_gate, unit_scale, 2.0 * unit_scale)
    offsets = jnp.where(is_gate, 0.0, -2.0 * unit_scale)
    weights = base_perp * column_scale[None, None, :] + direction[None, :, None] * offsets[None, None, :]
    return jnp.clip(weights, -2.0, 2.0).astype(jnp.bfloat16)


def touch_ends(array, own_key, low, high):
    longest = array.shape.index(max(array.shape))
    spots = []
    for shift in (0, 1):
        where = [jax.random.randint(jax.random.fold_in(own_key, axis), (), 0, length) for axis, length in enumerate(array.shape)]
        where[longest] = (where[longest] + shift) % array.shape[longest]
        spots.append(tuple(where))
    return array.at[spots[0]].set(low).at[spots[1]].set(high)


def levels(own_key, dims, pieces, low, largest):
    loudness, own = 1.0, jax.random.fold_in(own_key, 6)
    for position, blocks in pieces:
        draws = jnp.exp(jax.random.uniform(jax.random.fold_in(own, position), (blocks,), jnp.float32, low / len(pieces), largest / len(pieces)))
        loudness = loudness * jnp.repeat(draws, dims[position] // blocks).reshape([-1 if axis == position else 1 for axis in range(len(dims))])
    return loudness


def rank_bounds(number_of, lean):
    weights = [(1 << 20) // math.isqrt(rank ** lean) + 1 for rank in range(1, number_of + 1)]
    deviation = 1 + sum(weights) // (1 << 30)
    return np.cumsum(np.array([max(1, weight // deviation) for weight in weights]))


def ranked(own_key, dims, count, slope):
    table = rank_bounds(count, slope)
    pick = jax.random.randint(jax.random.fold_in(own_key, 1), dims, 0, int(table[count - 1]))
    standing = jnp.searchsorted(jnp.asarray(table, jnp.int32), pick, side="right")
    return jax.random.permutation(jax.random.fold_in(own_key, 2), count)[standing].astype(jnp.int32)


def split_up(number_of, total, bound, slope):
    weights = [(1 << 20) // math.isqrt(rank ** slope) + 1 for rank in range(2, number_of + 1)]
    spare, given = total - bound - (number_of - 1), [1] * (number_of - 1)
    while spare > 0:
        free = [i for i in range(number_of - 1) if given[i] < bound]
        mass, remaining = sum([weights[i] for i in free]), spare
        for i in free:
            addition = min(bound - given[i], max(1, remaining * weights[i] // mass), spare)
            given[i] = given[i] + addition
            spare = spare - addition
    return np.array([bound] + given)


def uneven_parts(rng, number_of, total, most, lean):
    if number_of == 2:
        one = jax.random.randint(rng, (), max(1, total - most), min(most, total - 1) + 1)
        return jnp.stack([one, total - one])
    tallies = jnp.asarray(split_up(number_of, total, most, lean), jnp.int32)
    couples = (number_of - 1) // 2
    giver, sink = tallies[1:1 + 2 * couples:2], tallies[2:2 + 2 * couples:2]
    slack = jnp.minimum(giver - 1, most - sink)
    passed = jax.random.randint(jax.random.fold_in(rng, 1), (couples,), 0, 1 << 20) % (slack + 1)
    tallies = tallies.at[1:1 + 2 * couples:2].set(giver - passed).at[2:2 + 2 * couples:2].set(sink + passed)
    return tallies[jax.random.permutation(jax.random.fold_in(rng, 2), number_of)]


def deal_out(own_key, own, number, rows, count, top, reach, slope):
    sequence = jax.random.permutation(own_key, count)
    heavy_load, common = shares(count, rows * top, reach, slope, True), shares(count, rows * top, reach, slope, False)
    places = jnp.arange(count)

    def named(sizes, turn):
        used = int((sizes > 0).sum())
        fixed = max(1, used // 4)
        moved = fixed + (places - fixed + turn * (used - fixed)) % max(1, count - fixed)
        return jnp.zeros((count,), jnp.int32).at[sequence[jnp.where(places < fixed, places, moved)]].set(jnp.asarray(sizes, jnp.int32))

    sizes = jnp.where(number % 4 == 0, named(heavy_load, number // 4), named(common, number - number // 4 - 1))
    mixed = jax.random.permutation(jax.random.fold_in(own, 3), count)
    donor, taker = mixed[0:count // 2 * 2:2], mixed[1:count // 2 * 2:2]
    room = jnp.minimum(sizes[donor] - 1, reach - sizes[taker]) // 2
    room = jnp.where((donor == sequence[0]) | (taker == sequence[0]) | (sizes[taker] == 0), 0, jnp.maximum(room, 0))
    moved = jax.random.randint(jax.random.fold_in(own, 4), (count // 2,), 0, 1 << 20) % (room + 1)
    sizes = sizes.at[donor].add(-moved).at[taker].add(moved)
    members = jnp.searchsorted(jnp.cumsum(sizes), jnp.arange(rows * top), side="right").astype(jnp.int32)
    table = members.reshape(top, rows).T
    table = table[jax.random.permutation(jax.random.fold_in(own, 1), rows)]
    turn = jax.random.randint(jax.random.fold_in(own, 2), (rows, 1), 0, top)
    return jnp.take_along_axis(table, (jnp.arange(top)[None, :] + turn) % top, axis=1)


def shares(number_of, total, most, skew, full):
    portions = [(1 << 20) // math.isqrt(rank ** skew) + 1 for rank in range(1, number_of + 1)]
    largest = most if full else min(most, max(-(-total // number_of), total * portions[0] // sum(portions)))
    least = 1 if total - largest >= number_of - 1 else 0
    given, rest = [largest] + [least] * (number_of - 1), total - largest - least * (number_of - 1)
    while rest > 0:
        movable = [i for i in range(1, number_of) if given[i] < largest] or [i for i in range(1, number_of) if given[i] < most]
        pool, budget = sum([portions[i] for i in movable]), rest
        for i in movable:
            more = min(most - given[i], max(1, budget * portions[i] // pool), rest)
            given[i] = given[i] + more
            rest = rest - more
    return np.array(given)


def centred(key, dims, deviation, bound, cuts=(), kind=jnp.bfloat16):
    result = jax.random.normal(key, dims, jnp.float32) * deviation
    if len(cuts) > 0:
        result = levels(key, dims, cuts, -0.22, 0.18) * result
    return jnp.clip(result, min=-bound, max=bound).astype(kind)


def setup_inputs(seed: int = 0) -> dict:
    streams_of = jax.random.split(jax.random.key(seed), 9)
    item_table = draw_item_table(jax.random.fold_in(streams_of[8], 71), 0)
    item_owner_keys = jax.random.split(jax.random.fold_in(streams_of[1], 1), N_EMB * MICRO * GROUP_TOK // TOK_DEV)
    item_owner_turns = jax.random.permutation(jax.random.fold_in(streams_of[1], 3), N_EMB * MICRO * GROUP_TOK // TOK_DEV)
    item_owner = jax.vmap(lambda own, number: deal_out(jax.random.fold_in(streams_of[1], 2), own, number, TOK_DEV, N_EMB, 1, CAP, 2))(item_owner_keys, item_owner_turns).reshape((N_EMB, MICRO, GROUP_TOK, 1))
    item_slot = touch_ends(ranked(streams_of[2], (N_EMB, MICRO, GROUP_TOK), V_DEV, 2), jax.random.fold_in(streams_of[2], 3), 0, V_DEV - 1).astype(jnp.int32)
    seq_lengths = jax.vmap(lambda own: uneven_parts(own, SEQS, GROUP_TOK, MAXLEN, 0))(jax.random.split(streams_of[3], N_EMB * MICRO)).reshape((N_EMB, MICRO, SEQS)).astype(jnp.int32)
    row_grads = centred(streams_of[4], (N_EMB, MICRO, GROUP_TOK, D), 1.0, 6.0, ((0, 4), (1, 2), (2, 16)))
    proj_weight = draw_proj_weight(jax.random.fold_in(streams_of[8], 71), 0)
    out_weight = centred(streams_of[6], (N_PHASE, HEADS * HEAD_DIM, D), (HEADS * HEAD_DIM) ** -0.5, 0.25, ((0, 2),))
    final_gain = jnp.clip(1.0 + 0.18 * jax.random.normal(streams_of[7], (D,), jnp.float32), 0.1, 1.9)
    return {"item_table": item_table, "item_owner": item_owner, "item_slot": item_slot, "seq_lengths": seq_lengths, "row_grads": row_grads, "proj_weight": proj_weight, "out_weight": out_weight, "final_gain": final_gain}


norm_eps = 1e-05

def layer_norm(values):
    average = lax.optimization_barrier(jnp.mean(values, axis=-1, keepdims=True))
    centered = values - average
    return centered * lax.rsqrt(lax.optimization_barrier(jnp.mean(centered * centered, axis=-1, keepdims=True)) + norm_eps)

def segment_of(positions, lengths):
    bounds = jnp.cumsum(lengths.astype(jnp.int32)).astype(jnp.int32)[:-1]
    return lax.optimization_barrier(jnp.sum((positions[:, None] >= bounds[None, :]).astype(jnp.int32), axis=1))

def section(inputs, proj_w, out_w, lengths):
    normed = layer_norm(inputs.astype(jnp.float32)).astype(jnp.bfloat16)
    activated = jax.nn.silu(jnp.dot(normed, proj_w, preferred_element_type=jnp.float32)).astype(jnp.bfloat16)
    inner_width = HEADS * HEAD_DIM
    gate_rows = activated[:, :inner_width]
    value_rows = activated[:, inner_width:2 * inner_width]
    query_rows = activated[:, 2 * inner_width:3 * inner_width]
    key_rows = activated[:, 3 * inner_width:]
    positions = jnp.arange(GROUP_TOK, dtype=jnp.int32)
    segments = segment_of(positions, lengths)
    visible = (positions[None, :] <= positions[:, None]) & (segments[None, :] == segments[:, None])
    query_heads = query_rows.reshape(GROUP_TOK, HEADS, HEAD_DIM).astype(jnp.float32)
    key_heads = key_rows.reshape(GROUP_TOK, HEADS, HEAD_DIM).astype(jnp.float32)
    value_heads = value_rows.reshape(GROUP_TOK, HEADS, HEAD_DIM).astype(jnp.float32)
    scores = jnp.einsum('qhd,khd->hqk', query_heads, key_heads)
    attn_weights = jnp.where(visible[None], jax.nn.silu(scores), 0.0).astype(jnp.bfloat16)
    mixed_heads = jnp.einsum('hqk,khd->qhd', attn_weights.astype(jnp.float32), value_heads).reshape(GROUP_TOK, inner_width)
    gated = (layer_norm(mixed_heads) * gate_rows.astype(jnp.float32)).astype(jnp.bfloat16)
    return inputs.astype(jnp.float32) + jnp.dot(gated, out_w, preferred_element_type=jnp.float32)

def reference(item_table, item_owner, item_slot, seq_lengths, row_grads, proj_weight, out_weight, final_gain):
    item_rows = (item_owner[..., 0] * V_DEV + item_slot).astype(jnp.int32)
    embedded = item_table[item_rows]

    def per_group(packed):
        group_rows, group_lengths = packed
        states = []
        for micro in range(MICRO):
            middle = section(group_rows[micro], proj_weight[0], out_weight[0], group_lengths[micro]).astype(jnp.bfloat16)
            closing = section(middle, proj_weight[1], out_weight[1], group_lengths[micro])
            states.append((layer_norm(closing) * final_gain).astype(jnp.bfloat16))
        return jnp.stack(states)
    sequence_states = lax.map(per_group, (embedded, seq_lengths))
    table_grad = jnp.zeros((VOCAB, D), jnp.float32).at[item_rows.reshape(-1)].add(row_grads.reshape(-1, D).astype(jnp.float32))
    return (sequence_states, table_grad)
```

```python
import functools

import jax
import jax.numpy as jnp
from jax import lax
from jax.experimental import pallas as pl
from jax.experimental.pallas import tpu as pltpu
from jax.sharding import PartitionSpec as P

MESH = pl.DeviceIdType.MESH
F32 = jnp.float32
BF16 = jnp.bfloat16
EPS = 1e-05
BIG = 2.0**40

TOK = 256
DIM = 512
HD = 128
CAP = 128
OWNED = 1024

KV_A, Q_A, HOP_R, HOP_L, FAR_K, FAR_V, MIX = 0, 3, 6, 10, 14, 18, 22
PER_SECTION = 25
REQ, ROWS, GRAD, WGT, OWGT, HALF, GA, GB = 50, 53, 56, 59, 60, 61, 62, 65
N_REMOTE = 68


def dot(left, right):
    return jnp.dot(left, right, preferred_element_type=F32)


def layer_norm(values):
    average = jnp.mean(values, axis=-1, keepdims=True)
    centered = values - average
    return centered * lax.rsqrt(jnp.mean(centered * centered, axis=-1, keepdims=True) + EPS)


def silu(v):
    u = 0.5 * v
    return u + u * jnp.tanh(u)


def iota(shape, dim):
    return lax.broadcasted_iota(jnp.int32, shape, dim)


def kernel(
    owner_ref, slot_ref, len_ref, gain_ref, table_hbm, grads_hbm, w_hbm, ow_hbm,
    states_ref, tg_ref,
    table, grads, w_all, ow_all, req_snd, req_rcv, rows_snd, rows_rcv, go_snd, g_rcv,
    x_ref, snd, gates, kv, qs, acc, mix_snd, mix, half_snd, half_own, half_rcv,
    ga_snd, ga_rcv, gb_snd, gb_rcv, ssem, rsem, lsem,
):
    ex = lax.axis_index("emb")
    row = lax.axis_index("row")
    c = lax.axis_index("phase")
    z, y = row // 4, row % 4
    a = z * (1 - c) + y * c
    b = y * (1 - c) + z * c
    sa, sb = 4 - 3 * c, 1 + 3 * c

    def at_a(d):
        return {"row": sa * ((a + d) % 4) + sb * b}

    def at_b(d):
        return {"row": sa * a + sb * ((b + d) % 4)}

    def at_x(d):
        return {"emb": (ex + d) % 4}

    other = {"phase": 1 - c}

    def rc(src, dst, sem, dev):
        return pltpu.make_async_remote_copy(
            src_ref=src, dst_ref=dst, send_sem=ssem.at[sem], recv_sem=rsem.at[sem],
            device_id=dev, device_id_type=MESH,
        )

    cp_table = pltpu.make_async_copy(table_hbm, table, lsem.at[0])
    cp_grads = pltpu.make_async_copy(grads_hbm, grads, lsem.at[1])
    cp_w = pltpu.make_async_copy(w_hbm, w_all.at[c], lsem.at[2])
    cp_ow = pltpu.make_async_copy(ow_hbm, ow_all.at[c], lsem.at[3])
    for cp in (cp_table, cp_grads, cp_w, cp_ow):
        cp.start()
    barrier = pltpu.get_barrier_semaphore()
    for d in (1, 2, 3):
        for dev in (at_x(d), at_a(d), at_b(d)):
            pl.semaphore_signal(barrier, inc=1, device_id=dev, device_id_type=MESH)
    pl.semaphore_signal(barrier, inc=1, device_id=other, device_id_type=MESH)

    own_row = owner_ref[...].astype(F32)
    slot_row = slot_ref[...].astype(F32)
    ti, tj = iota((TOK, TOK), 0), iota((TOK, TOK), 1)
    eye = ti == tj
    own_col = jnp.sum(jnp.where(eye, own_row, 0.0), axis=1, keepdims=True)
    slot_col = jnp.sum(jnp.where(eye, slot_row, 0.0), axis=1, keepdims=True)
    same = own_col == own_row
    rank_col = jnp.sum(jnp.where(same & (tj < ti), 1.0, 0.0), axis=1, keepdims=True)
    rank_row = jnp.sum(jnp.where(same & (ti < tj), 1.0, 0.0), axis=0, keepdims=True)
    key_col = (own_col * CAP + rank_col).astype(jnp.int32)
    key_row = (own_row * CAP + rank_row).astype(jnp.int32)
    place = key_col == iota((TOK, 4 * CAP), 1)
    req_row = jnp.sum(jnp.where(place, slot_col + 1.0, 0.0), axis=0, keepdims=True) - 1.0
    for e in range(4):
        req_snd[e] = jnp.broadcast_to(req_row[:, e * CAP : (e + 1) * CAP], (8, CAP))
    cp_req = pltpu.make_async_copy(req_snd.at[ex], req_rcv.at[ex], lsem.at[4])
    cp_req.start()
    pl.semaphore_wait(barrier, 10)
    req = [rc(req_snd.at[(ex + d) % 4], req_rcv.at[ex], REQ + d - 1, at_x(d)) for d in (1, 2, 3)]
    for d in (2, 1, 3):
        req[d - 1].start()
    wgt = rc(w_hbm, w_all.at[c], WGT, other)
    owgt = rc(ow_hbm, ow_all.at[c], OWGT, other)
    wgt.start()
    owgt.start()

    cp_grads.wait()
    place_t = (key_row == iota((4 * CAP, TOK), 0)).astype(F32).astype(BF16)
    for e in range(4):
        go_snd[e] = dot(place_t[e * CAP : (e + 1) * CAP], grads[...]).astype(BF16)
    cp_go = pltpu.make_async_copy(go_snd.at[ex], g_rcv.at[ex], lsem.at[5])
    cp_go.start()

    cp_req.wait()
    cp_table.wait()
    eye_cap = iota((CAP, CAP), 0) == iota((CAP, CAP), 1)

    def look_up(q):
        wanted = jnp.sum(
            jnp.where(eye_cap, req_rcv[q][0:1], 0.0), axis=1, keepdims=True
        ).astype(jnp.int32)
        picked = (wanted == iota((CAP, OWNED), 1)).astype(F32).astype(BF16)
        rows_snd[q] = dot(picked, table[...]).astype(BF16)

    rows = [rc(rows_snd.at[(ex + d) % 4], rows_rcv.at[ex], ROWS + d - 1, at_x(d)) for d in (1, 2, 3)]
    for d in (3, 1, 2):
        req[d - 1].wait_recv()
        look_up((ex + 4 - d) % 4)
        rows[3 - d].start()
    look_up(ex)
    cp_rows = pltpu.make_async_copy(rows_snd.at[ex], rows_rcv.at[ex], lsem.at[6])
    cp_rows.start()
    cp_rows.wait()
    for d in (1, 2, 3):
        rows[d - 1].wait_recv()
    embedded = dot(
        place.astype(F32).astype(BF16), rows_rcv[...].reshape(4 * CAP, DIM)
    )
    x_ref[...] = embedded.astype(BF16)

    grad = [rc(go_snd.at[(ex + d) % 4], g_rcv.at[ex], GRAD + d - 1, at_x(d)) for d in (1, 2, 3)]
    for d in (2, 1, 3):
        grad[d - 1].start()
    cp_w.wait()
    cp_ow.wait()
    wgt.wait_recv()
    owgt.wait_recv()

    bound = len_ref[c, 0]
    lane0 = iota((TOK, HD), 1) == 0
    pos = iota((TOK, HD), 0)
    diff = ti - tj

    def partial_half(cc):
        j = iota((512, 1), 0)
        aj, bj, i = j // 128, (j // 32) % 4, j % 32
        slot = ((4 - 3 * cc) * aj + (1 + 3 * cc) * bj) * 64 + cc * 32 + i
        total = None
        for q in range(4):
            hit = (slot == req_rcv[q][0:1].astype(jnp.int32)).astype(F32).astype(BF16)
            term = dot(hit, g_rcv[q])
            total = term if total is None else total + term
        return total

    half = rc(half_snd, half_rcv, HALF, other)
    ga = [rc(ga_snd.at[(a + d) % 4], ga_rcv.at[a], GA + d - 1, at_a(d)) for d in (1, 2, 3)]
    gb = [rc(gb_snd.at[(b + d) % 4], gb_rcv.at[b], GB + d - 1, at_b(d)) for d in (1, 2, 3)]

    for s in (0, 1):
        base = s * PER_SECTION
        normed = layer_norm(x_ref[...].astype(F32)).astype(BF16)
        kv_a = [rc(snd.at[(a + d) % 4, pl.ds(0, 2)], kv.at[s, b, a], base + KV_A + d - 1, at_a(d)) for d in (1, 2, 3)]
        q_a = [rc(snd.at[(a + d) % 4, 2], qs.at[s, a], base + Q_A + d - 1, at_a(d)) for d in (1, 2, 3)]
        mixs = [rc(mix_snd.at[(a + d) % 4], mix.at[s, a], base + MIX + d - 1, at_a(d)) for d in (1, 2, 3)]

        def hop_r(i, base=base, s=s):
            block = kv.at[s, b, (a + 4 - i) % 4]
            return rc(block, block, base + HOP_R + i, at_b(1))

        def hop_l(i, base=base, s=s):
            block = kv.at[s, b, (a + 4 - i) % 4]
            return rc(block, block, base + HOP_L + i, at_b(3))

        def far_k(i, base=base, s=s):
            block = kv.at[s, (b + 3) % 4, (a + 4 - i) % 4, 0]
            return rc(block, block, base + FAR_K + i, at_b(1))

        def far_v(i, base=base, s=s):
            block = kv.at[s, (b + 1) % 4, (a + 4 - i) % 4, 1]
            return rc(block, block, base + FAR_V + i, at_b(3))

        def project(part, column, scale):
            made = silu(dot(normed, w_all[s, :, column : column + DIM])) * scale
            for h in range(4):
                snd[h, part] = made[:, h * HD : (h + 1) * HD].astype(BF16)

        project(0, 1536, 1.0)
        project(1, 512, 1.0)
        for d in (2, 1, 3):
            kv_a[d - 1].start()
        cp_kv = pltpu.make_async_copy(snd.at[a, pl.ds(0, 2)], kv.at[s, b, a], lsem.at[7])
        cp_kv.start()
        cp_kv.wait()
        hop_r(0).start()
        hop_l(0).start()
        project(2, 1024, 0.5)
        for d in (2, 1, 3):
            q_a[d - 1].start()
        cp_q = pltpu.make_async_copy(snd.at[a, 2], qs.at[s, a], lsem.at[8])
        cp_q.start()
        for d in (1, 2, 3):
            kv_a[d - 1].wait_recv()
            hop_r(d).start()
            hop_l(d).start()
        gates[...] = silu(dot(normed, w_all[s, :, 0:DIM])).astype(BF16)
        acc[...] = jnp.zeros_like(acc)
        if s == 1:
            half.wait_recv()
            summed = half_own[...] + half_rcv[...].astype(F32)
            half_own[...] = summed
            for k in range(4):
                ga_snd[k] = summed[k * 128 : (k + 1) * 128].astype(BF16)
            for d in (2, 1, 3):
                ga[d - 1].start()
        cp_q.wait()
        for d in (1, 2, 3):
            q_a[d - 1].wait_recv()

        def attend(bb, aa, s=s):
            key_row0 = 256 * (sa * aa + sb * bb)
            before = (pos + key_row0 < bound) & lane0
            keys = jnp.concatenate(
                [kv[s, bb, aa, 0], jnp.where(before, 1.0, 0.0).astype(BF16)], axis=1
            )
            values = kv[s, bb, aa, 1]
            for k in range(4):
                query_row0 = 256 * (sa * k + sb * b)
                after = (pos + query_row0 >= bound) & lane0
                queries = jnp.concatenate(
                    [qs[s, k], jnp.where(after, -BIG, 0.0).astype(BF16)], axis=1
                )
                u = lax.dot_general(
                    queries, keys, (((1,), (1,)), ((), ())), preferred_element_type=F32
                )
                weights = jnp.where(diff >= key_row0 - query_row0, u + u * jnp.tanh(u), 0.0)
                acc[k] += dot(weights.astype(BF16), values)

        def step(n, carry):
            stage, i = n // 4, n % 4

            @pl.when(stage == 0)
            def _():
                hop_r(i).wait_recv()
                far_k(i).start()
                hop_l(i).wait_recv()
                far_v(i).start()

            @pl.when(stage == 3)
            def _():
                far_k(i).wait_recv()
                far_v(i).wait_recv()

            turn = 3 * (stage % 2) + (stage // 2) * (1 - stage % 2) - (stage // 3)
            bb = (b + turn) % 4

            @pl.when((c == 0) | (bb <= b))
            def _():
                attend(bb, (a + 4 - i) % 4)

            return carry

        lax.fori_loop(0, 16, step, 0)
        for k in range(4):
            mix_snd[k] = acc[k].astype(BF16)
        for d in (2, 1, 3):
            mixs[d - 1].start()
        cp_mix = pltpu.make_async_copy(mix_snd.at[a], mix.at[s, a], lsem.at[9])
        cp_mix.start()

        if s == 0:
            cp_go.wait()
            for d in (1, 2, 3):
                grad[d - 1].wait_recv()
            half_snd[...] = partial_half(1 - c).astype(BF16)
            half.start()
            half_own[...] = partial_half(c)
        else:
            for d in (1, 2, 3):
                ga[d - 1].wait_recv()
            total = half_own[pl.ds(pl.multiple_of(a * 128, 128), 128), :]
            for d in (1, 2, 3):
                total = total + ga_rcv[(a + d) % 4].astype(F32)
            half_own[0:128, :] = total
            for k in range(4):
                gb_snd[k] = total[k * 32 : (k + 1) * 32].astype(BF16)
            for d in (2, 1, 3):
                gb[d - 1].start()

        cp_mix.wait()
        for d in (1, 2, 3):
            mixs[d - 1].wait_recv()
        mixed = jnp.concatenate([mix[s, h] for h in range(4)], axis=1).astype(F32)
        gated = (layer_norm(mixed) * gates[...].astype(F32)).astype(BF16)
        residual = x_ref[...].astype(F32) + dot(gated, ow_all[s])
        if s == 0:
            x_ref[...] = residual.astype(BF16)
        else:
            states_ref[...] = (layer_norm(residual) * gain_ref[...]).astype(BF16)
        for d in (1, 2, 3):
            kv_a[d - 1].wait_send()
            q_a[d - 1].wait_send()
            mixs[d - 1].wait_send()

        def drain(i, carry):
            hop_r(i).wait_send()
            hop_l(i).wait_send()
            far_k(i).wait_send()
            far_v(i).wait_send()
            return carry

        lax.fori_loop(0, 4, drain, 0)

    for d in (1, 2, 3):
        gb[d - 1].wait_recv()
    total = half_own[pl.ds(pl.multiple_of(b * 32, 32), 32), :]
    for d in (1, 2, 3):
        total = total + gb_rcv[(b + d) % 4].astype(F32)
    tg_ref[...] = total
    for cp in req + rows + grad + [wgt, owgt, half] + ga + gb:
        cp.wait_send()


def body(
    item_table, item_owner, item_slot, seq_lengths, row_grads, proj_weight, out_weight, final_gain
):
    vmem = pl.BlockSpec(memory_space=pltpu.VMEM)
    hbm = pl.BlockSpec(memory_space=pl.ANY)
    smem = pl.BlockSpec(memory_space=pltpu.SMEM)

    def buf(*shape, dtype=BF16):
        return pltpu.VMEM(shape, dtype)

    states, table_grad = pl.pallas_call(
        kernel,
        out_shape=(
            jax.ShapeDtypeStruct((TOK, DIM), BF16),
            jax.ShapeDtypeStruct((32, DIM), F32),
        ),
        in_specs=[vmem, vmem, smem, vmem, hbm, hbm, hbm, hbm],
        out_specs=(vmem, vmem),
        scratch_shapes=[
            buf(OWNED, DIM), buf(TOK, DIM), buf(2, DIM, 4 * DIM), buf(2, DIM, DIM),
            buf(4, 8, CAP, dtype=F32), buf(4, 8, CAP, dtype=F32),
            buf(4, CAP, DIM), buf(4, CAP, DIM), buf(4, CAP, DIM), buf(4, CAP, DIM),
            buf(TOK, DIM), buf(4, 3, TOK, HD), buf(TOK, DIM),
            buf(2, 4, 4, 2, TOK, HD), buf(2, 4, TOK, HD), buf(4, TOK, HD, dtype=F32),
            buf(4, TOK, HD), buf(2, 4, TOK, HD),
            buf(512, DIM), buf(512, DIM, dtype=F32), buf(512, DIM),
            buf(4, 128, DIM), buf(4, 128, DIM), buf(4, 32, DIM), buf(4, 32, DIM),
            pltpu.SemaphoreType.DMA((N_REMOTE,)),
            pltpu.SemaphoreType.DMA((N_REMOTE,)),
            pltpu.SemaphoreType.DMA((10,)),
        ],
        compiler_params=pltpu.CompilerParams(
            collective_id=0, has_side_effects=True, vmem_limit_bytes=56 << 20
        ),
    )(
        item_owner.reshape(1, TOK),
        item_slot.reshape(1, TOK),
        seq_lengths.reshape(2, 2),
        final_gain.reshape(1, DIM),
        item_table,
        row_grads.reshape(TOK, DIM),
        proj_weight.reshape(DIM, 4 * DIM),
        out_weight.reshape(DIM, DIM),
    )
    return states.reshape(1, 1, TOK, DIM), table_grad


def solution(mesh):
    placed = (
        P("emb", None),
        P("emb", "phase", "row", None),
        P("emb", "phase", "row"),
        P("emb", None, None),
        P("emb", "phase", "row", None),
        P("phase", None, None),
        P("phase", None, None),
        P(),
    )
    return jax.shard_map(
        body,
        mesh=mesh,
        in_specs=placed,
        out_specs=(P("emb", "phase", "row", None), P(("emb", "row", "phase"), None)),
        check_vma=False,
    )
```

```python
import functools

import jax
import jax.numpy as jnp
from jax import lax
from jax.experimental import pallas as pl
from jax.experimental.pallas import tpu as pltpu
from jax.sharding import PartitionSpec as P

MESH = pl.DeviceIdType.MESH
F32 = jnp.float32
BF16 = jnp.bfloat16
EPS = 1e-05
BIG = 2.0**40

TOK = 256
DIM = 512
HD = 128
CAP = 128
OWNED = 1024

KV_A, Q_A, HOP_R, HOP_L, FAR_K, FAR_V, MIX = 0, 3, 6, 10, 14, 18, 22
PER_SECTION = 25
REQ, ROWS, GRAD, WGT, OWGT, HALF, GA, GB = 50, 53, 56, 59, 60, 61, 62, 65
N_REMOTE = 68


def dot(left, right):
    return jnp.dot(left, right, preferred_element_type=F32)


def layer_norm(values):
    average = jnp.mean(values, axis=-1, keepdims=True)
    centered = values - average
    return centered * lax.rsqrt(jnp.mean(centered * centered, axis=-1, keepdims=True) + EPS)


def silu(v):
    u = 0.5 * v
    return u + u * jnp.tanh(u)


def iota(shape, dim):
    return lax.broadcasted_iota(jnp.int32, shape, dim)


def kernel(
    owner_ref, slot_ref, len_ref, gain_ref, table_hbm, grads_hbm, w_hbm, ow_hbm,
    states_ref, tg_ref,
    table, grads, w_all, ow_all, req_snd, req_rcv, rows_snd, rows_rcv, go_snd, g_rcv,
    x_ref, snd, gates, kv, qs, acc, mix_snd, mix, half_snd, half_own, half_rcv,
    ga_snd, ga_rcv, gb_snd, gb_rcv, q_ext, k_ext, diff_ref, ssem, rsem, lsem,
):
    ex = lax.axis_index("emb")
    row = lax.axis_index("row")
    c = lax.axis_index("phase")
    z, y = row // 4, row % 4
    a = z * (1 - c) + y * c
    b = y * (1 - c) + z * c
    sa, sb = 4 - 3 * c, 1 + 3 * c

    def at_a(d):
        return {"row": sa * ((a + d) % 4) + sb * b}

    def at_b(d):
        return {"row": sa * a + sb * ((b + d) % 4)}

    def at_x(d):
        return {"emb": (ex + d) % 4}

    other = {"phase": 1 - c}

    def rc(src, dst, sem, dev):
        return pltpu.make_async_remote_copy(
            src_ref=src, dst_ref=dst, send_sem=ssem.at[sem], recv_sem=rsem.at[sem],
            device_id=dev, device_id_type=MESH,
        )

    cp_table = pltpu.make_async_copy(table_hbm, table, lsem.at[0])
    cp_grads = pltpu.make_async_copy(grads_hbm, grads, lsem.at[1])
    cp_w = pltpu.make_async_copy(w_hbm, w_all.at[c], lsem.at[2])
    cp_ow = pltpu.make_async_copy(ow_hbm, ow_all.at[c], lsem.at[3])
    for cp in (cp_table, cp_grads, cp_w, cp_ow):
        cp.start()
    barrier = pltpu.get_barrier_semaphore()
    for d in (1, 2, 3):
        for dev in (at_x(d), at_a(d), at_b(d)):
            pl.semaphore_signal(barrier, inc=1, device_id=dev, device_id_type=MESH)
    pl.semaphore_signal(barrier, inc=1, device_id=other, device_id_type=MESH)

    own_row = owner_ref[...].astype(F32)
    slot_row = slot_ref[...].astype(F32)
    ti, tj = iota((TOK, TOK), 0), iota((TOK, TOK), 1)
    eye = ti == tj
    own_col = jnp.sum(jnp.where(eye, own_row, 0.0), axis=1, keepdims=True)
    slot_col = jnp.sum(jnp.where(eye, slot_row, 0.0), axis=1, keepdims=True)
    same = own_col == own_row
    rank_col = jnp.sum(jnp.where(same & (tj < ti), 1.0, 0.0), axis=1, keepdims=True)
    rank_row = jnp.sum(jnp.where(same & (ti < tj), 1.0, 0.0), axis=0, keepdims=True)
    key_col = (own_col * CAP + rank_col).astype(jnp.int32)
    key_row = (own_row * CAP + rank_row).astype(jnp.int32)
    place = key_col == iota((TOK, 4 * CAP), 1)
    req_row = jnp.sum(jnp.where(place, slot_col + 1.0, 0.0), axis=0, keepdims=True) - 1.0
    for e in range(4):
        req_snd[e] = jnp.broadcast_to(req_row[:, e * CAP : (e + 1) * CAP], (8, CAP))
    cp_req = pltpu.make_async_copy(req_snd.at[ex], req_rcv.at[ex], lsem.at[4])
    cp_req.start()
    bound = len_ref[c, 0]
    lane0 = iota((TOK, HD), 1) == 0
    pos = iota((TOK, HD), 0)
    diff_ref[...] = ti - tj
    for k in range(4):
        after = (pos + 256 * (sa * k + sb * b) >= bound) & lane0
        q_ext[k] = jnp.where(after, -BIG, 0.0).astype(BF16)
        for h in range(4):
            before = (pos + 256 * (sa * k + sb * h) < bound) & lane0
            k_ext[h, k] = jnp.where(before, 1.0, 0.0).astype(BF16)
    pl.semaphore_wait(barrier, 10)
    req = [rc(req_snd.at[(ex + d) % 4], req_rcv.at[ex], REQ + d - 1, at_x(d)) for d in (1, 2, 3)]
    for d in (2, 1, 3):
        req[d - 1].start()
    wgt = rc(w_hbm, w_all.at[c], WGT, other)
    owgt = rc(ow_hbm, ow_all.at[c], OWGT, other)
    wgt.start()
    owgt.start()

    cp_grads.wait()
    place_t = (key_row == iota((4 * CAP, TOK), 0)).astype(F32).astype(BF16)
    for e in range(4):
        go_snd[e] = dot(place_t[e * CAP : (e + 1) * CAP], grads[...]).astype(BF16)
    cp_go = pltpu.make_async_copy(go_snd.at[ex], g_rcv.at[ex], lsem.at[5])
    cp_go.start()

    cp_req.wait()
    cp_table.wait()
    eye_cap = iota((CAP, CAP), 0) == iota((CAP, CAP), 1)

    def look_up(q):
        wanted = jnp.sum(
            jnp.where(eye_cap, req_rcv[q][0:1], 0.0), axis=1, keepdims=True
        ).astype(jnp.int32)
        picked = (wanted == iota((CAP, OWNED), 1)).astype(F32).astype(BF16)
        rows_snd[q] = dot(picked, table[...]).astype(BF16)

    rows = [rc(rows_snd.at[(ex + d) % 4], rows_rcv.at[ex], ROWS + d - 1, at_x(d)) for d in (1, 2, 3)]
    look_up(ex)
    cp_rows = pltpu.make_async_copy(rows_snd.at[ex], rows_rcv.at[ex], lsem.at[6])
    cp_rows.start()
    for d in (1, 3, 2):
        req[d - 1].wait_recv()
        look_up((ex + 4 - d) % 4)
        rows[3 - d].start()
    cp_rows.wait()
    for d in (1, 2, 3):
        rows[d - 1].wait_recv()
    embedded = dot(
        place.astype(F32).astype(BF16), rows_rcv[...].reshape(4 * CAP, DIM)
    )
    x_ref[...] = embedded.astype(BF16)

    grad = [rc(go_snd.at[(ex + d) % 4], g_rcv.at[ex], GRAD + d - 1, at_x(d)) for d in (1, 2, 3)]
    for d in (2, 1, 3):
        grad[d - 1].start()
    cp_w.wait()
    cp_ow.wait()
    wgt.wait_recv()
    owgt.wait_recv()

    def partial_half(cc):
        j = iota((512, 1), 0)
        aj, bj, i = j // 128, (j // 32) % 4, j % 32
        slot = ((4 - 3 * cc) * aj + (1 + 3 * cc) * bj) * 64 + cc * 32 + i
        total = None
        for q in range(4):
            hit = (slot == req_rcv[q][0:1].astype(jnp.int32)).astype(F32).astype(BF16)
            term = dot(hit, g_rcv[q])
            total = term if total is None else total + term
        return total

    half = rc(half_snd, half_rcv, HALF, other)
    ga = [rc(ga_snd.at[(a + d) % 4], ga_rcv.at[a], GA + d - 1, at_a(d)) for d in (1, 2, 3)]
    gb = [rc(gb_snd.at[(b + d) % 4], gb_rcv.at[b], GB + d - 1, at_b(d)) for d in (1, 2, 3)]

    def kv_a(s, d):
        return rc(snd.at[s, (a + d) % 4, pl.ds(0, 2)], kv.at[s, b, a], s * PER_SECTION + KV_A + d - 1, at_a(d))

    def q_a(s, d):
        return rc(snd.at[s, (a + d) % 4, 2], qs.at[s, a], s * PER_SECTION + Q_A + d - 1, at_a(d))

    def mix_a(s, d):
        return rc(mix_snd.at[s, (a + d) % 4], mix.at[s, a], s * PER_SECTION + MIX + d - 1, at_a(d))

    def hop_r(s, r):
        block = kv.at[s, b, r]
        return rc(block, block, s * PER_SECTION + HOP_R + r, at_b(1))

    def hop_l(s, r):
        block = kv.at[s, b, r]
        return rc(block, block, s * PER_SECTION + HOP_L + r, at_b(3))

    def hop_v(s, r):
        block = kv.at[s, b, r, 1]
        return rc(block, block, s * PER_SECTION + HOP_L + r, at_b(3))

    def far_k(s, r):
        block = kv.at[s, (b + 3) % 4, r, 0]
        return rc(block, block, s * PER_SECTION + FAR_K + r, at_b(1))

    def far_kv(s, r):
        block = kv.at[s, (b + 3) % 4, r]
        return rc(block, block, s * PER_SECTION + FAR_K + r, at_b(1))

    def far_v(s, r):
        block = kv.at[s, (b + 1) % 4, r, 1]
        return rc(block, block, s * PER_SECTION + FAR_V + r, at_b(3))

    uses_l = (c == 0) | (b > 0)
    uses_r = (c == 0) | (b == 3)
    sends_r = (c == 0) | (b < 3)
    sends_l = (c == 0) | (b == 0)
    sends_v = (c == 1) & (b == 1)
    sends_far_k = (c == 0) | (b == 2)
    sends_far_kv = (c == 1) & (b == 1)
    sends_far_v = (c == 0) | (b == 0)

    def start_hops(s, r):
        @pl.when(sends_r)
        def _():
            hop_r(s, r).start()

        @pl.when(sends_l)
        def _():
            hop_l(s, r).start()

        @pl.when(sends_v)
        def _():
            hop_v(s, r).start()

    def take_left(s, r):
        @pl.when(uses_l)
        def _():
            hop_r(s, r).wait_recv()

        @pl.when(sends_far_k)
        def _():
            far_k(s, r).start()

        @pl.when(sends_far_kv)
        def _():
            far_kv(s, r).start()

    def take_right(s, r):
        @pl.when(uses_r)
        def _():
            hop_l(s, r).wait_recv()

        @pl.when((c == 1) & (b == 0))
        def _():
            hop_v(s, r).wait_recv()

        @pl.when(sends_far_v)
        def _():
            far_v(s, r).start()

    def take_far(s, r):
        @pl.when(uses_r)
        def _():
            far_k(s, r).wait_recv()
            far_v(s, r).wait_recv()

        @pl.when((c == 1) & (b == 2))
        def _():
            far_kv(s, r).wait_recv()

    def section_start(s):
        normed = layer_norm(x_ref[...].astype(F32)).astype(BF16)

        def project(part, column, scale):
            made = silu(dot(normed, w_all[s, :, column : column + DIM])) * scale
            for h in range(4):
                snd[s, h, part] = made[:, h * HD : (h + 1) * HD].astype(BF16)

        project(0, 1536, 1.0)
        project(1, 512, 1.0)
        for d in (1, 3):
            kv_a(s, d).start()
        cp_kv = pltpu.make_async_copy(snd.at[s, a, pl.ds(0, 2)], kv.at[s, b, a], lsem.at[7])
        cp_kv.start()
        cp_kv.wait()

        @pl.when(c == 0)
        def _():
            start_hops(s, a)

        project(2, 1024, 0.5)
        cp_q = pltpu.make_async_copy(snd.at[s, a, 2], qs.at[s, a], lsem.at[8])
        cp_q.start()
        gates[...] = silu(dot(normed, w_all[s, :, 0:DIM])).astype(BF16)
        cp_q.wait()
        kv_a(s, 1).wait_send()
        kv_a(s, 3).wait_send()
        kv_a(s, 2).start()
        for d in (1, 3, 2):
            q_a(s, d).start()

    def section_end(s):
        for d in (1, 2, 3):
            mix_a(s, d).wait_recv()
        mixed = jnp.concatenate([mix[s, h] for h in range(4)], axis=1).astype(F32)
        gated = (layer_norm(mixed) * gates[...].astype(F32)).astype(BF16)
        return x_ref[...].astype(F32) + dot(gated, ow_all[s])

    def send_mix(s, r):
        @pl.when(r == a)
        def _():
            mix[s, a] = acc[r].astype(BF16)

        @pl.when(r != a)
        def _():
            mix_snd[s, r] = acc[r].astype(BF16)
            mix_a(s, (r + 4 - a) % 4).start()

    def attend(s, bb, rows, firsts):
        terms = []
        for r, first in zip(rows, firsts):
            keys = jnp.concatenate([kv[s, bb, r, 0], k_ext[bb, r]], axis=1)
            m = (4 - first) * TOK
            queries = jnp.concatenate(
                [qs[s, first:4].reshape(m, HD), q_ext[first:4].reshape(m, HD)], axis=1
            )
            u = lax.dot_general(
                queries, keys, (((1,), (1,)), ((), ())), preferred_element_type=F32
            )
            weights = u + u * jnp.tanh(u)
            ahead = 256 * (sa * r + sb * bb) - 256 * (sa * first + sb * b)
            head = jnp.where(diff_ref[...] >= ahead, weights[:TOK], 0.0)
            weights = jnp.concatenate([head, weights[TOK:]], axis=0) if first < 3 else head
            terms.append(dot(weights.astype(BF16), kv[s, bb, r, 1]))
        low, high = firsts
        apart = (high - low) * TOK
        if apart:
            acc[low:high] += terms[0][:apart].reshape(high - low, TOK, HD)
        acc[high:4] += (terms[0][apart:] + terms[1]).reshape(4 - high, TOK, HD)

    def grad_partials():
        for d in (1, 2, 3):
            grad[d - 1].wait_recv()
        half_snd[...] = partial_half(1 - c).astype(BF16)
        half.start()
        half_own[...] = partial_half(c)

    def grad_stage_a():
        half.wait_recv()
        summed = half_own[...] + half_rcv[...].astype(F32)
        half_own[...] = summed
        for k in range(4):
            ga_snd[k] = summed[k * 128 : (k + 1) * 128].astype(BF16)
        for d in (2, 1, 3):
            ga[d - 1].start()

    def grad_stage_b():
        for d in (1, 2, 3):
            ga[d - 1].wait_recv()
        total = half_own[pl.ds(pl.multiple_of(a * 128, 128), 128), :]
        for d in (1, 2, 3):
            total = total + ga_rcv[(a + d) % 4].astype(F32)
        half_own[0:128, :] = total
        for k in range(4):
            gb_snd[k] = total[k * 32 : (k + 1) * 32].astype(BF16)
        for d in (2, 1, 3):
            gb[d - 1].start()

    def section(s, carry):
        @pl.when(s == 1)
        def _():
            x_ref[...] = section_end(0).astype(BF16)

        section_start(s)
        acc[...] = jnp.zeros_like(acc)
        for d in (1, 3, 2):
            kv_a(s, d).wait_recv()

            @pl.when(c == 0)
            def _(d=d):
                start_hops(s, (a + 4 - d) % 4)

        @pl.when(c == 1)
        def _():
            for d in (0, 1, 3, 2):
                start_hops(s, (a + 4 - d) % 4)

        for d in (1, 3, 2):
            q_a(s, d).wait_recv()

        take_left(s, a)
        take_right(s, a)

        def take_pair(take, p):
            for k in (0, 1):

                @pl.when(2 * p + k != a)
                def _(k=k):
                    take(s, 2 * p + k)

        def step(n, carry):
            own, far = n < 2, n >= 6
            side = n % 2
            p = jnp.where(own, n, jnp.where(far, n - 6, (n - 2) // 2))
            bb = (b + jnp.where(own, 0, jnp.where(far, 2, 3 - 2 * side))) % 4
            near = (n >= 2) & (n < 6)

            @pl.when(near & (side == 0))
            def _():
                take_pair(take_left, p)
                take_pair(take_right, p)

            @pl.when((s == 1) & (n == 6))
            def _():
                grad_stage_a()

            @pl.when(far)
            def _():
                take_far(s, 2 * p)
                take_far(s, 2 * p + 1)

            split = (c == 0) | (bb == b)

            @pl.when(split & (p == 0))
            def _():
                attend(s, bb, (0, 1), (0, 1))

            @pl.when(split & (p == 1))
            def _():
                attend(s, bb, (2, 3), (2, 3))

            @pl.when((c == 1) & (bb < b))
            def _():
                attend(s, bb, (2 * p, 2 * p + 1), (0, 0))

            return carry

        lax.fori_loop(0, 8, step, 0)
        for r in range(4):
            send_mix(s, r)

        @pl.when(s == 0)
        def _():
            grad_partials()

        return carry

    cp_go.wait()
    lax.fori_loop(0, 2, section, 0)
    grad_stage_b()
    states_ref[...] = (layer_norm(section_end(1)) * gain_ref[...]).astype(BF16)

    for s in (0, 1):
        for d in (1, 2, 3):
            if d == 2:
                kv_a(s, d).wait_send()
            q_a(s, d).wait_send()
            mix_a(s, d).wait_send()

    def drain(n, carry):
        s, r = n // 4, n % 4
        for used, copy in (
            (sends_r, hop_r), (sends_l, hop_l), (sends_v, hop_v),
            (sends_far_k, far_k), (sends_far_kv, far_kv), (sends_far_v, far_v),
        ):

            @pl.when(used)
            def _(copy=copy):
                copy(s, r).wait_send()

        return carry

    lax.fori_loop(0, 8, drain, 0)

    for d in (1, 2, 3):
        gb[d - 1].wait_recv()
    total = half_own[pl.ds(pl.multiple_of(b * 32, 32), 32), :]
    for d in (1, 2, 3):
        total = total + gb_rcv[(b + d) % 4].astype(F32)
    tg_ref[...] = total
    for cp in req + rows + grad + [wgt, owgt, half] + ga + gb:
        cp.wait_send()


def body(
    item_table, item_owner, item_slot, seq_lengths, row_grads, proj_weight, out_weight, final_gain
):
    vmem = pl.BlockSpec(memory_space=pltpu.VMEM)
    hbm = pl.BlockSpec(memory_space=pl.ANY)
    smem = pl.BlockSpec(memory_space=pltpu.SMEM)

    def buf(*shape, dtype=BF16):
        return pltpu.VMEM(shape, dtype)

    states, table_grad = pl.pallas_call(
        kernel,
        out_shape=(
            jax.ShapeDtypeStruct((TOK, DIM), BF16),
            jax.ShapeDtypeStruct((32, DIM), F32),
        ),
        in_specs=[vmem, vmem, smem, vmem, hbm, hbm, hbm, hbm],
        out_specs=(vmem, vmem),
        scratch_shapes=[
            buf(OWNED, DIM), buf(TOK, DIM), buf(2, DIM, 4 * DIM), buf(2, DIM, DIM),
            buf(4, 8, CAP, dtype=F32), buf(4, 8, CAP, dtype=F32),
            buf(4, CAP, DIM), buf(4, CAP, DIM), buf(4, CAP, DIM), buf(4, CAP, DIM),
            buf(TOK, DIM), buf(2, 4, 3, TOK, HD), buf(TOK, DIM),
            buf(2, 4, 4, 2, TOK, HD), buf(2, 4, TOK, HD), buf(4, TOK, HD, dtype=F32),
            buf(2, 4, TOK, HD), buf(2, 4, TOK, HD),
            buf(512, DIM), buf(512, DIM, dtype=F32), buf(512, DIM),
            buf(4, 128, DIM), buf(4, 128, DIM), buf(4, 32, DIM), buf(4, 32, DIM),
            buf(4, TOK, HD), buf(4, 4, TOK, HD), buf(TOK, TOK, dtype=jnp.int32),
            pltpu.SemaphoreType.DMA((N_REMOTE,)),
            pltpu.SemaphoreType.DMA((N_REMOTE,)),
            pltpu.SemaphoreType.DMA((10,)),
        ],
        compiler_params=pltpu.CompilerParams(
            collective_id=0, has_side_effects=True, vmem_limit_bytes=56 << 20
        ),
    )(
        item_owner.reshape(1, TOK),
        item_slot.reshape(1, TOK),
        seq_lengths.reshape(2, 2),
        final_gain.reshape(1, DIM),
        item_table,
        row_grads.reshape(TOK, DIM),
        proj_weight.reshape(DIM, 4 * DIM),
        out_weight.reshape(DIM, DIM),
    )
    return states.reshape(1, 1, TOK, DIM), table_grad


def solution(mesh):
    placed = (
        P("emb", None),
        P("emb", "phase", "row", None),
        P("emb", "phase", "row"),
        P("emb", None, None),
        P("emb", "phase", "row", None),
        P("phase", None, None),
        P("phase", None, None),
        P(),
    )
    return jax.shard_map(
        body,
        mesh=mesh,
        in_specs=placed,
        out_specs=(P("emb", "phase", "row", None), P(("emb", "row", "phase"), None)),
        check_vma=False,
    )
```

```python
import functools

import jax
import jax.numpy as jnp
from jax import lax
from jax.experimental import pallas as pl
from jax.experimental.pallas import tpu as pltpu
from jax.sharding import PartitionSpec as P

MESH = pl.DeviceIdType.MESH
F32 = jnp.float32
BF16 = jnp.bfloat16
EPS = 1e-05
BIG = 2.0**40

TOK = 256
DIM = 512
HD = 128
CAP = 128
OWNED = 1024

KV_A, Q_A, HOP_R, HOP_L, FAR, MIX = 0, 3, 4, 8, 12, 16
PER_SECTION = 17
REQ, ROWS, GRAD, WGT, OWGT, HALF, GA, GB = 34, 37, 38, 39, 40, 41, 42, 43
N_RECV = 44
S_KV, _, S_Q, S_R, S_L, S_FK, S_FV, S_MIX = range(8)
SENDS = 8
S_REQ, S_ROWS, S_GRAD, S_WGT, S_OWGT, S_HALF, S_GA, S_GB = range(16, 24)
N_SEND = 24


def dot(left, right):
    return jnp.dot(left, right, preferred_element_type=F32)


def layer_norm(values):
    average = jnp.mean(values, axis=-1, keepdims=True)
    centered = values - average
    return centered * lax.rsqrt(jnp.mean(centered * centered, axis=-1, keepdims=True) + EPS)


def silu(v):
    u = 0.5 * v
    return u + u * jnp.tanh(u)


def iota(shape, dim):
    return lax.broadcasted_iota(jnp.int32, shape, dim)


def kernel(
    owner_ref, slot_ref, len_ref, gain_ref, table_hbm, grads_hbm, w_hbm, ow_hbm,
    states_ref, tg_ref,
    table, grads, w_all, ow_all, req_snd, req_rcv, rows_snd, rows_rcv, go_snd, g_rcv,
    x_ref, snd, gates, kv, qs, acc, mix_snd, mix, half_snd, half_own, half_rcv,
    ga_snd, ga_rcv, gb_snd, gb_rcv, q_ext, k_ext, diff_ref, ssem, rsem, lsem,
):
    ex = lax.axis_index("emb")
    row = lax.axis_index("row")
    c = lax.axis_index("phase")
    z, y = row // 4, row % 4
    a = z * (1 - c) + y * c
    b = y * (1 - c) + z * c
    sa, sb = 4 - 3 * c, 1 + 3 * c

    def at_a(d):
        return {"row": sa * ((a + d) % 4) + sb * b}

    def at_b(d):
        return {"row": sa * a + sb * ((b + d) % 4)}

    def at_x(d):
        return {"emb": (ex + d) % 4}

    other = {"phase": 1 - c}

    def rc(src, dst, left, came, dev):
        return pltpu.make_async_remote_copy(
            src_ref=src, dst_ref=dst, send_sem=ssem.at[left], recv_sem=rsem.at[came],
            device_id=dev, device_id_type=MESH,
        )

    def all_of(ref, left, came):
        return rc(ref, ref, left, came, other)

    cp_table = pltpu.make_async_copy(table_hbm, table, lsem.at[0])
    cp_grads = pltpu.make_async_copy(grads_hbm, grads, lsem.at[1])
    cp_w = pltpu.make_async_copy(w_hbm, w_all.at[c], lsem.at[2])
    cp_ow = pltpu.make_async_copy(ow_hbm, ow_all.at[c], lsem.at[3])
    for cp in (cp_table, cp_grads, cp_w, cp_ow):
        cp.start()
    barrier = pltpu.get_barrier_semaphore()
    for d in (1, 2, 3):
        for dev in (at_x(d), at_a(d), at_b(d)):
            pl.semaphore_signal(barrier, inc=1, device_id=dev, device_id_type=MESH)
    pl.semaphore_signal(barrier, inc=1, device_id=other, device_id_type=MESH)

    own_row = owner_ref[...].astype(F32)
    slot_row = slot_ref[...].astype(F32)
    ti, tj = iota((TOK, TOK), 0), iota((TOK, TOK), 1)
    eye = ti == tj
    own_col = jnp.sum(jnp.where(eye, own_row, 0.0), axis=1, keepdims=True)
    slot_col = jnp.sum(jnp.where(eye, slot_row, 0.0), axis=1, keepdims=True)
    same = own_col == own_row
    rank_col = jnp.sum(jnp.where(same & (tj < ti), 1.0, 0.0), axis=1, keepdims=True)
    rank_row = jnp.sum(jnp.where(same & (ti < tj), 1.0, 0.0), axis=0, keepdims=True)
    key_col = (own_col * CAP + rank_col).astype(jnp.int32)
    key_row = (own_row * CAP + rank_row).astype(jnp.int32)
    place = key_col == iota((TOK, 4 * CAP), 1)
    req_row = jnp.sum(jnp.where(place, slot_col + 1.0, 0.0), axis=0, keepdims=True) - 1.0
    for e in range(4):
        req_snd[e] = jnp.broadcast_to(req_row[:, e * CAP : (e + 1) * CAP], (8, CAP))
    cp_req = pltpu.make_async_copy(req_snd.at[ex], req_rcv.at[ex], lsem.at[4])
    cp_req.start()
    bound = len_ref[c, 0]
    lane0 = iota((TOK, HD), 1) == 0
    pos = iota((TOK, HD), 0)
    diff_ref[...] = ti - tj
    for k in range(4):
        after = (pos + 256 * (sa * k + sb * b) >= bound) & lane0
        q_ext[k] = jnp.where(after, -BIG, 0.0).astype(BF16)
        for h in range(4):
            before = (pos + 256 * (sa * k + sb * h) < bound) & lane0
            k_ext[h, k] = jnp.where(before, 1.0, 0.0).astype(BF16)
    pl.semaphore_wait(barrier, 10)
    req = [rc(req_snd.at[(ex + d) % 4], req_rcv.at[ex], S_REQ, REQ + d - 1, at_x(d)) for d in (1, 2, 3)]
    for d in (2, 1, 3):
        req[d - 1].start()
    wgt = rc(w_hbm, w_all.at[c], S_WGT, WGT, other)
    owgt = rc(ow_hbm, ow_all.at[c], S_OWGT, OWGT, other)
    wgt.start()
    owgt.start()

    cp_grads.wait()
    place_t = (key_row == iota((4 * CAP, TOK), 0)).astype(F32).astype(BF16)
    for e in range(4):
        go_snd[e] = dot(place_t[e * CAP : (e + 1) * CAP], grads[...]).astype(BF16)
    cp_go = pltpu.make_async_copy(go_snd.at[ex], g_rcv.at[ex], lsem.at[5])
    cp_go.start()

    cp_req.wait()
    cp_table.wait()
    eye_cap = iota((CAP, CAP), 0) == iota((CAP, CAP), 1)

    def look_up(q):
        wanted = jnp.sum(
            jnp.where(eye_cap, req_rcv[q][0:1], 0.0), axis=1, keepdims=True
        ).astype(jnp.int32)
        picked = (wanted == iota((CAP, OWNED), 1)).astype(F32).astype(BF16)
        rows_snd[q] = dot(picked, table[...]).astype(BF16)

    rows = [rc(rows_snd.at[(ex + d) % 4], rows_rcv.at[ex], S_ROWS, ROWS, at_x(d)) for d in (1, 2, 3)]
    look_up(ex)
    cp_rows = pltpu.make_async_copy(rows_snd.at[ex], rows_rcv.at[ex], lsem.at[6])
    cp_rows.start()
    for d in (1, 3, 2):
        req[d - 1].wait_recv()
        look_up((ex + 4 - d) % 4)
        rows[3 - d].start()
    cp_rows.wait()
    all_of(rows_rcv.at[pl.ds(0, 3)], S_ROWS, ROWS).wait_recv()
    embedded = dot(
        place.astype(F32).astype(BF16), rows_rcv[...].reshape(4 * CAP, DIM)
    )
    x_ref[...] = embedded.astype(BF16)

    grad = [rc(go_snd.at[(ex + d) % 4], g_rcv.at[ex], S_GRAD, GRAD, at_x(d)) for d in (1, 2, 3)]
    for d in (2, 1, 3):
        grad[d - 1].start()
    cp_w.wait()
    cp_ow.wait()
    wgt.wait_recv()
    owgt.wait_recv()

    def partial_half(cc):
        j = iota((512, 1), 0)
        aj, bj, i = j // 128, (j // 32) % 4, j % 32
        slot = ((4 - 3 * cc) * aj + (1 + 3 * cc) * bj) * 64 + cc * 32 + i
        total = None
        for q in range(4):
            hit = (slot == req_rcv[q][0:1].astype(jnp.int32)).astype(F32).astype(BF16)
            term = dot(hit, g_rcv[q])
            total = term if total is None else total + term
        return total

    half = rc(half_snd, half_rcv, S_HALF, HALF, other)
    ga = [rc(ga_snd.at[(a + d) % 4], ga_rcv.at[a], S_GA, GA, at_a(d)) for d in (1, 2, 3)]
    gb = [rc(gb_snd.at[(b + d) % 4], gb_rcv.at[b], S_GB, GB, at_b(d)) for d in (1, 2, 3)]

    def kv_a(s, d):
        return rc(snd.at[s, (a + d) % 4, pl.ds(0, 2)], kv.at[s, b, a], s * SENDS + S_KV + 1 - d % 2, s * PER_SECTION + KV_A + d - 1, at_a(d))

    def q_a(s, d):
        return rc(snd.at[s, (a + d) % 4, 2], qs.at[s, a], s * SENDS + S_Q, s * PER_SECTION + Q_A, at_a(d))

    def mix_a(s, d):
        return rc(mix_snd.at[s, (a + d) % 4], mix.at[s, a], s * SENDS + S_MIX, s * PER_SECTION + MIX, at_a(d))

    def hop_r(s, r):
        block = kv.at[s, b, r]
        return rc(block, block, s * SENDS + S_R, s * PER_SECTION + HOP_R + r, at_b(1))

    def hop_l(s, r):
        block = kv.at[s, b, r]
        return rc(block, block, s * SENDS + S_L, s * PER_SECTION + HOP_L + r, at_b(3))

    def hop_v(s, r):
        block = kv.at[s, b, r, 1]
        return rc(block, block, s * SENDS + S_L, s * PER_SECTION + HOP_L + r, at_b(3))

    def far_k(s, r):
        block = kv.at[s, (b + 3) % 4, r, 0]
        return rc(block, block, s * SENDS + S_FK, s * PER_SECTION + FAR + r, at_b(1))

    def far_kv(s, r):
        block = kv.at[s, (b + 3) % 4, r]
        return rc(block, block, s * SENDS + S_FK, s * PER_SECTION + FAR + r, at_b(1))

    def far_v(s, r):
        block = kv.at[s, (b + 1) % 4, r, 1]
        return rc(block, block, s * SENDS + S_FV, s * PER_SECTION + FAR + r, at_b(3))

    uses_l = (c == 0) | (b > 0)
    uses_r = (c == 0) | (b == 3)
    sends_r = (c == 0) | (b < 3)
    sends_l = (c == 0) | (b == 0)
    sends_v = (c == 1) & (b == 1)
    sends_far_k = (c == 0) | (b == 2)
    sends_far_kv = (c == 1) & (b == 1)
    sends_far_v = (c == 0) | (b == 0)

    def start_hops(s, r):
        @pl.when(sends_r)
        def _():
            hop_r(s, r).start()

        @pl.when(sends_l)
        def _():
            hop_l(s, r).start()

        @pl.when(sends_v)
        def _():
            hop_v(s, r).start()

    def take_left(s, r):
        @pl.when(uses_l)
        def _():
            hop_r(s, r).wait_recv()

        @pl.when(sends_far_k)
        def _():
            far_k(s, r).start()

        @pl.when(sends_far_kv)
        def _():
            far_kv(s, r).start()

    def take_right(s, r):
        @pl.when(uses_r)
        def _():
            hop_l(s, r).wait_recv()

        @pl.when((c == 1) & (b == 0))
        def _():
            hop_v(s, r).wait_recv()

        @pl.when(sends_far_v)
        def _():
            far_v(s, r).start()

    def take_far(s, r):
        @pl.when(uses_r)
        def _():
            all_of(kv.at[s, b, r], s * SENDS + S_FK, s * PER_SECTION + FAR + r).wait_recv()

        @pl.when((c == 1) & (b == 2))
        def _():
            far_kv(s, r).wait_recv()

    def section_start(s):
        normed = layer_norm(x_ref[...].astype(F32)).astype(BF16)

        def project(part, column, scale):
            made = silu(dot(normed, w_all[s, :, column : column + DIM])) * scale
            for h in range(4):
                snd[s, h, part] = made[:, h * HD : (h + 1) * HD].astype(BF16)

        project(0, 1536, 1.0)
        project(1, 512, 1.0)
        for d in (1, 3):
            kv_a(s, d).start()
        cp_kv = pltpu.make_async_copy(snd.at[s, a, pl.ds(0, 2)], kv.at[s, b, a], lsem.at[7])
        cp_kv.start()
        cp_kv.wait()

        @pl.when(c == 0)
        def _():
            start_hops(s, a)

        project(2, 1024, 0.5)
        cp_q = pltpu.make_async_copy(snd.at[s, a, 2], qs.at[s, a], lsem.at[8])
        cp_q.start()
        gates[...] = silu(dot(normed, w_all[s, :, 0:DIM])).astype(BF16)
        cp_q.wait()
        all_of(kv.at[s, b, pl.ds(0, 2)], s * SENDS + S_KV, 0).wait_send()
        for d in (1, 3, 2):
            q_a(s, d).start()
        kv_a(s, 2).start()

    def section_end(s):
        all_of(mix.at[s, pl.ds(0, 3)], s * SENDS + S_MIX, s * PER_SECTION + MIX).wait_recv()
        mixed = jnp.concatenate([mix[s, h] for h in range(4)], axis=1).astype(F32)
        gated = (layer_norm(mixed) * gates[...].astype(F32)).astype(BF16)
        return x_ref[...].astype(F32) + dot(gated, ow_all[s])

    def send_mix(s, r):
        @pl.when(r == a)
        def _():
            mix[s, a] = acc[r].astype(BF16)

        @pl.when(r != a)
        def _():
            mix_snd[s, r] = acc[r].astype(BF16)
            mix_a(s, (r + 4 - a) % 4).start()

    def attend(s, first, blocks):
        m = (4 - first) * TOK
        queries = jnp.concatenate(
            [qs[s, first:4].reshape(m, HD), q_ext[first:4].reshape(m, HD)], axis=1
        )
        total = None
        for bb, r, masked in blocks:
            keys = jnp.concatenate([kv[s, bb, r, 0], k_ext[bb, r]], axis=1)
            u = lax.dot_general(
                queries, keys, (((1,), (1,)), ((), ())), preferred_element_type=F32
            )
            weights = u + u * jnp.tanh(u)
            parts = []
            for k in range(masked):
                ahead = 256 * (sa * r + sb * bb) - 256 * (sa * (first + k) + sb * b)
                part = weights[k * TOK : (k + 1) * TOK]
                parts.append(jnp.where(diff_ref[...] >= ahead, part, 0.0))
            if masked:
                if first + masked < 4:
                    parts.append(weights[masked * TOK :])
                weights = jnp.concatenate(parts, axis=0)
            term = dot(weights.astype(BF16), kv[s, bb, r, 1])
            total = term if total is None else total + term
        acc[first:4] += total.reshape(4 - first, TOK, HD)

    def grad_partials():
        all_of(g_rcv.at[pl.ds(0, 3)], S_GRAD, GRAD).wait_recv()
        half_snd[...] = partial_half(1 - c).astype(BF16)
        half.start()
        half_own[...] = partial_half(c)

    def grad_stage_a():
        half.wait_recv()
        summed = half_own[...] + half_rcv[...].astype(F32)
        half_own[...] = summed
        for k in range(4):
            ga_snd[k] = summed[k * 128 : (k + 1) * 128].astype(BF16)
        for d in (2, 1, 3):
            ga[d - 1].start()

    def grad_stage_b():
        all_of(ga_rcv.at[pl.ds(0, 3)], S_GA, GA).wait_recv()
        total = half_own[pl.ds(pl.multiple_of(a * 128, 128), 128), :]
        for d in (1, 2, 3):
            total = total + ga_rcv[(a + d) % 4].astype(F32)
        half_own[0:128, :] = total
        for k in range(4):
            gb_snd[k] = total[k * 32 : (k + 1) * 32].astype(BF16)
        for d in (2, 1, 3):
            gb[d - 1].start()

    def section(s, carry):
        @pl.when(s == 1)
        def _():
            x_ref[...] = section_end(0).astype(BF16)

        section_start(s)
        acc[...] = jnp.zeros_like(acc)
        odd = a % 2
        pair = a // 2
        mate, next_row, last_row = a + 1 - 2 * odd, (a + 3 + 2 * odd) % 4, (a + 2) % 4
        for d in (3 - 2 * odd, 1 + 2 * odd):
            kv_a(s, d).wait_recv()

            @pl.when(c == 0)
            def _(d=d):
                start_hops(s, (a + 4 - d) % 4)

        @pl.when(c == 0)
        def _():
            take_left(s, a)
            take_right(s, a)

        all_of(qs.at[s, pl.ds(0, 3)], s * SENDS + S_Q, s * PER_SECTION + Q_A).wait_recv()

        @pl.when(c == 1)
        def _():
            for r in (a, mate, next_row):
                start_hops(s, r)

        kv_a(s, 2).wait_recv()
        start_hops(s, last_row)

        takes = {
            0: ((0, mate),),
            1: ((0, next_row), (1, a)),
            2: ((1, mate),),
            3: ((0, last_row), (1, next_row)),
            4: ((1, last_row),),
        }
        for n, (kind, second) in enumerate(
            ((0, 0), (0, 1), (1, 0), (2, 0), (1, 1), (2, 1), (3, 0), (3, 1))
        ):
            p = 1 - pair if second else pair
            bb = (b + (0, 3, 1, 2)[kind]) % 4

            for core, r in takes.get(n, ()):

                @pl.when(c == core)
                def _(r=r):
                    take_left(s, r)
                    take_right(s, r)

            if n in (0, 2):

                @pl.when((s == 1) & (c == 1 - n // 2))
                def _():
                    grad_stage_a()

            if kind == 3:
                take_far(s, 2 * p)
                take_far(s, 2 * p + 1)

            split = (p >= 0) if kind == 0 else (c == 0)

            @pl.when(split & (p == 0))
            def _(bb=bb):
                attend(s, 0, ((bb, 0, 1), (bb, 1, 2)))

            @pl.when(split & (p == 1))
            def _(bb=bb):
                attend(s, 2, ((bb, 2, 1), (bb, 3, 2)))

            if kind:

                @pl.when((c == 1) & (bb < b))
                def _(bb=bb, p=p):
                    attend(s, 0, ((bb, 2 * p, 0), (bb, 2 * p + 1, 0)))

        for r in range(4):
            send_mix(s, r)

        @pl.when(s == 0)
        def _():
            grad_partials()

        return carry

    cp_go.wait()
    lax.fori_loop(0, 2, section, 0)
    grad_stage_b()
    states_ref[...] = (layer_norm(section_end(1)) * gain_ref[...]).astype(BF16)

    for s in (0, 1):
        kv_a(s, 2).wait_send()
        all_of(qs.at[s, pl.ds(0, 3)], s * SENDS + S_Q, 0).wait_send()
        all_of(mix.at[s, pl.ds(0, 3)], s * SENDS + S_MIX, 0).wait_send()
        whole, part = kv.at[s, b], kv.at[s, b, pl.ds(0, 2)]
        for used, ref, left in (
            (sends_r, whole, S_R), (sends_l, whole, S_L), (sends_v, part, S_L),
            (sends_far_k, part, S_FK), (sends_far_kv, whole, S_FK), (sends_far_v, part, S_FV),
        ):

            @pl.when(used)
            def _(ref=ref, left=left, s=s):
                all_of(ref, s * SENDS + left, 0).wait_send()

    all_of(gb_rcv.at[pl.ds(0, 3)], S_GB, GB).wait_recv()
    total = half_own[pl.ds(pl.multiple_of(b * 32, 32), 32), :]
    for d in (1, 2, 3):
        total = total + gb_rcv[(b + d) % 4].astype(F32)
    tg_ref[...] = total
    for ref, left in (
        (req_rcv, S_REQ), (rows_rcv, S_ROWS), (g_rcv, S_GRAD), (ga_rcv, S_GA), (gb_rcv, S_GB),
    ):
        all_of(ref.at[pl.ds(0, 3)], left, 0).wait_send()
    for cp in (wgt, owgt, half):
        cp.wait_send()


def body(
    item_table, item_owner, item_slot, seq_lengths, row_grads, proj_weight, out_weight, final_gain
):
    vmem = pl.BlockSpec(memory_space=pltpu.VMEM)
    hbm = pl.BlockSpec(memory_space=pl.ANY)
    smem = pl.BlockSpec(memory_space=pltpu.SMEM)

    def buf(*shape, dtype=BF16):
        return pltpu.VMEM(shape, dtype)

    states, table_grad = pl.pallas_call(
        kernel,
        out_shape=(
            jax.ShapeDtypeStruct((TOK, DIM), BF16),
            jax.ShapeDtypeStruct((32, DIM), F32),
        ),
        in_specs=[vmem, vmem, smem, vmem, hbm, hbm, hbm, hbm],
        out_specs=(vmem, vmem),
        scratch_shapes=[
            buf(OWNED, DIM), buf(TOK, DIM), buf(2, DIM, 4 * DIM), buf(2, DIM, DIM),
            buf(4, 8, CAP, dtype=F32), buf(4, 8, CAP, dtype=F32),
            buf(4, CAP, DIM), buf(4, CAP, DIM), buf(4, CAP, DIM), buf(4, CAP, DIM),
            buf(TOK, DIM), buf(2, 4, 3, TOK, HD), buf(TOK, DIM),
            buf(2, 4, 4, 2, TOK, HD), buf(2, 4, TOK, HD), buf(4, TOK, HD, dtype=F32),
            buf(2, 4, TOK, HD), buf(2, 4, TOK, HD),
            buf(512, DIM), buf(512, DIM, dtype=F32), buf(512, DIM),
            buf(4, 128, DIM), buf(4, 128, DIM), buf(4, 32, DIM), buf(4, 32, DIM),
            buf(4, TOK, HD), buf(4, 4, TOK, HD), buf(TOK, TOK, dtype=jnp.int32),
            pltpu.SemaphoreType.DMA((N_SEND,)),
            pltpu.SemaphoreType.DMA((N_RECV,)),
            pltpu.SemaphoreType.DMA((10,)),
        ],
        compiler_params=pltpu.CompilerParams(
            collective_id=0, has_side_effects=True, vmem_limit_bytes=56 << 20
        ),
    )(
        item_owner.reshape(1, TOK),
        item_slot.reshape(1, TOK),
        seq_lengths.reshape(2, 2),
        final_gain.reshape(1, DIM),
        item_table,
        row_grads.reshape(TOK, DIM),
        proj_weight.reshape(DIM, 4 * DIM),
        out_weight.reshape(DIM, DIM),
    )
    def hand_out(states_in, grad_in, states_out, grad_out):
        states_out[...] = states_in[...]
        grad_out[...] = grad_in[...]

    states, table_grad = pl.pallas_call(
        hand_out,
        out_shape=(
            jax.ShapeDtypeStruct((TOK, DIM), BF16),
            jax.ShapeDtypeStruct((32, DIM), F32),
        ),
        in_specs=[vmem, vmem],
        out_specs=(vmem, vmem),
    )(states, table_grad)
    return states.reshape(1, 1, TOK, DIM), table_grad


def solution(mesh):
    placed = (
        P("emb", None),
        P("emb", "phase", "row", None),
        P("emb", "phase", "row"),
        P("emb", None, None),
        P("emb", "phase", "row", None),
        P("phase", None, None),
        P("phase", None, None),
        P(),
    )
    return jax.shard_map(
        body,
        mesh=mesh,
        in_specs=placed,
        out_specs=(P("emb", "phase", "row", None), P(("emb", "row", "phase"), None)),
        check_vma=False,
    )
```

```python
import functools

import jax
import jax.numpy as jnp
from jax import lax
from jax.experimental import pallas as pl
from jax.experimental.pallas import tpu as pltpu
from jax.sharding import PartitionSpec as P

MESH = pl.DeviceIdType.MESH
F32 = jnp.float32
BF16 = jnp.bfloat16
EPS = 1e-05
BIG = 2.0**40

TOK = 256
DIM = 512
HD = 128
CAP = 128
OWNED = 1024

KV_A, Q_A, HOP_R, HOP_L, FAR, MIX = 0, 3, 4, 8, 12, 16
PER_SECTION = 17
REQ, ROWS, GRAD, WGT, OWGT, HALF, GA, GB = 34, 37, 38, 39, 40, 41, 42, 43
N_RECV = 44
S_KV, _, S_Q, S_R, S_L, S_FK, S_FV, S_MIX = range(8)
SENDS = 8
S_REQ, S_ROWS, S_GRAD, S_WGT, S_OWGT, S_HALF, S_GA, S_GB = range(16, 24)
N_SEND = 24


def dot(left, right):
    return jnp.dot(left, right, preferred_element_type=F32)


def layer_norm(values):
    average = jnp.mean(values, axis=-1, keepdims=True)
    centered = values - average
    return centered * lax.rsqrt(jnp.mean(centered * centered, axis=-1, keepdims=True) + EPS)


def silu(v):
    u = 0.5 * v
    return u + u * jnp.tanh(u)


def iota(shape, dim):
    return lax.broadcasted_iota(jnp.int32, shape, dim)


def kernel(
    owner_hbm, slot_hbm, len_hbm, gain_hbm, table_hbm, grads_hbm, w_hbm, ow_hbm,
    states_ref, tg_ref,
    owner_ref, slot_ref, len_ref, gain_ref, table, grads, w_all, ow_all, req_snd, req_rcv, rows_snd, rows_rcv, go_snd, g_rcv,
    x_ref, snd, gates, kv, qs, acc, mix_snd, mix, half_snd, half_own, half_rcv,
    ga_snd, ga_rcv, gb_snd, gb_rcv, q_ext, k_ext, diff_ref, ssem, rsem, lsem,
):
    ex = lax.axis_index("emb")
    row = lax.axis_index("row")
    c = lax.axis_index("phase")
    z, y = row // 4, row % 4
    a = z * (1 - c) + y * c
    b = y * (1 - c) + z * c
    sa, sb = 4 - 3 * c, 1 + 3 * c

    def at_a(d):
        return {"row": sa * ((a + d) % 4) + sb * b}

    def at_b(d):
        return {"row": sa * a + sb * ((b + d) % 4)}

    def at_x(d):
        return {"emb": (ex + d) % 4}

    other = {"phase": 1 - c}

    def rc(src, dst, left, came, dev):
        return pltpu.make_async_remote_copy(
            src_ref=src, dst_ref=dst, send_sem=ssem.at[left], recv_sem=rsem.at[came],
            device_id=dev, device_id_type=MESH,
        )

    def all_of(ref, left, came):
        return rc(ref, ref, left, came, other)

    barrier = pltpu.get_barrier_semaphore()
    for d in (1, 2, 3):
        for dev in (at_x(d), at_a(d), at_b(d)):
            pl.semaphore_signal(barrier, inc=1, device_id=dev, device_id_type=MESH)
    pl.semaphore_signal(barrier, inc=1, device_id=other, device_id_type=MESH)
    small = [
        pltpu.make_async_copy(src, dst, lsem.at[4 + k])
        for k, (src, dst) in enumerate(
            (
                (owner_hbm, owner_ref), (slot_hbm, slot_ref), (len_hbm, len_ref),
                (gain_hbm, gain_ref),
            )
        )
    ]
    for cp in small:
        cp.start()
    cp_table = pltpu.make_async_copy(table_hbm, table, lsem.at[0])
    cp_grads = pltpu.make_async_copy(grads_hbm, grads, lsem.at[1])
    cp_w = pltpu.make_async_copy(w_hbm, w_all.at[c], lsem.at[2])
    cp_ow = pltpu.make_async_copy(ow_hbm, ow_all.at[c], lsem.at[3])
    for cp in (cp_table, cp_grads, cp_w, cp_ow):
        cp.start()
    for cp in small:
        cp.wait()

    own_row = owner_ref[...].astype(F32)
    slot_row = slot_ref[...].astype(F32)
    ti, tj = iota((TOK, TOK), 0), iota((TOK, TOK), 1)
    eye = ti == tj
    own_col = jnp.sum(jnp.where(eye, own_row, 0.0), axis=1, keepdims=True)
    slot_col = jnp.sum(jnp.where(eye, slot_row, 0.0), axis=1, keepdims=True)
    same = own_col == own_row
    rank_col = jnp.sum(jnp.where(same & (tj < ti), 1.0, 0.0), axis=1, keepdims=True)
    rank_row = jnp.sum(jnp.where(same & (ti < tj), 1.0, 0.0), axis=0, keepdims=True)
    key_col = (own_col * CAP + rank_col).astype(jnp.int32)
    key_row = (own_row * CAP + rank_row).astype(jnp.int32)
    place = key_col == iota((TOK, 4 * CAP), 1)
    req_row = jnp.sum(jnp.where(place, slot_col + 1.0, 0.0), axis=0, keepdims=True) - 1.0
    for e in range(4):
        req_snd[e] = jnp.broadcast_to(req_row[:, e * CAP : (e + 1) * CAP], (8, CAP))
    cp_req = pltpu.make_async_copy(req_snd.at[ex], req_rcv.at[ex], lsem.at[4])
    cp_req.start()
    bound = len_ref[c, 0]
    lane0 = iota((TOK, HD), 1) == 0
    pos = iota((TOK, HD), 0)
    diff_ref[...] = ti - tj
    for k in range(4):
        after = (pos + 256 * (sa * k + sb * b) >= bound) & lane0
        q_ext[k] = jnp.where(after, -BIG, 0.0).astype(BF16)
        for h in range(4):
            before = (pos + 256 * (sa * k + sb * h) < bound) & lane0
            k_ext[h, k] = jnp.where(before, 1.0, 0.0).astype(BF16)
    pl.semaphore_wait(barrier, 10)
    req = [rc(req_snd.at[(ex + d) % 4], req_rcv.at[ex], S_REQ, REQ + d - 1, at_x(d)) for d in (1, 2, 3)]
    for d in (2, 1, 3):
        req[d - 1].start()
    wgt = rc(w_hbm, w_all.at[c], S_WGT, WGT, other)
    owgt = rc(ow_hbm, ow_all.at[c], S_OWGT, OWGT, other)
    wgt.start()
    owgt.start()

    cp_grads.wait()
    place_t = (key_row == iota((4 * CAP, TOK), 0)).astype(F32).astype(BF16)
    for e in range(4):
        go_snd[e] = dot(place_t[e * CAP : (e + 1) * CAP], grads[...]).astype(BF16)
    cp_go = pltpu.make_async_copy(go_snd.at[ex], g_rcv.at[ex], lsem.at[5])
    cp_go.start()

    cp_req.wait()
    cp_table.wait()
    eye_cap = iota((CAP, CAP), 0) == iota((CAP, CAP), 1)

    def look_up(q):
        wanted = jnp.sum(
            jnp.where(eye_cap, req_rcv[q][0:1], 0.0), axis=1, keepdims=True
        ).astype(jnp.int32)
        picked = (wanted == iota((CAP, OWNED), 1)).astype(F32).astype(BF16)
        rows_snd[q] = dot(picked, table[...]).astype(BF16)

    rows = [rc(rows_snd.at[(ex + d) % 4], rows_rcv.at[ex], S_ROWS, ROWS, at_x(d)) for d in (1, 2, 3)]
    look_up(ex)
    cp_rows = pltpu.make_async_copy(rows_snd.at[ex], rows_rcv.at[ex], lsem.at[6])
    cp_rows.start()
    for d in (1, 3, 2):
        req[d - 1].wait_recv()
        look_up((ex + 4 - d) % 4)
        rows[3 - d].start()
    cp_rows.wait()
    all_of(rows_rcv.at[pl.ds(0, 3)], S_ROWS, ROWS).wait_recv()
    embedded = dot(
        place.astype(F32).astype(BF16), rows_rcv[...].reshape(4 * CAP, DIM)
    )
    x_ref[...] = embedded.astype(BF16)

    grad = [rc(go_snd.at[(ex + d) % 4], g_rcv.at[ex], S_GRAD, GRAD, at_x(d)) for d in (1, 2, 3)]
    for d in (2, 1, 3):
        grad[d - 1].start()
    cp_w.wait()
    cp_ow.wait()
    wgt.wait_recv()
    owgt.wait_recv()

    def partial_half(cc):
        j = iota((512, 1), 0)
        aj, bj, i = j // 128, (j // 32) % 4, j % 32
        slot = ((4 - 3 * cc) * aj + (1 + 3 * cc) * bj) * 64 + cc * 32 + i
        total = None
        for q in range(4):
            hit = (slot == req_rcv[q][0:1].astype(jnp.int32)).astype(F32).astype(BF16)
            term = dot(hit, g_rcv[q])
            total = term if total is None else total + term
        return total

    half = rc(half_snd, half_rcv, S_HALF, HALF, other)
    ga = [rc(ga_snd.at[(a + d) % 4], ga_rcv.at[a], S_GA, GA, at_a(d)) for d in (1, 2, 3)]
    gb = [rc(gb_snd.at[(b + d) % 4], gb_rcv.at[b], S_GB, GB, at_b(d)) for d in (1, 2, 3)]

    def kv_a(s, d):
        return rc(snd.at[s, (a + d) % 4, pl.ds(0, 2)], kv.at[s, b, a], s * SENDS + S_KV + 1 - d % 2, s * PER_SECTION + KV_A + d - 1, at_a(d))

    def q_a(s, d):
        return rc(snd.at[s, (a + d) % 4, 2], qs.at[s, a], s * SENDS + S_Q, s * PER_SECTION + Q_A, at_a(d))

    def mix_a(s, d):
        return rc(mix_snd.at[s, (a + d) % 4], mix.at[s, a], s * SENDS + S_MIX, s * PER_SECTION + MIX, at_a(d))

    def hop_r(s, r):
        block = kv.at[s, b, r]
        return rc(block, block, s * SENDS + S_R, s * PER_SECTION + HOP_R + r, at_b(1))

    def hop_l(s, r):
        block = kv.at[s, b, r]
        return rc(block, block, s * SENDS + S_L, s * PER_SECTION + HOP_L + r, at_b(3))

    def hop_v(s, r):
        block = kv.at[s, b, r, 1]
        return rc(block, block, s * SENDS + S_L, s * PER_SECTION + HOP_L + r, at_b(3))

    def far_k(s, r):
        block = kv.at[s, (b + 3) % 4, r, 0]
        return rc(block, block, s * SENDS + S_FK, s * PER_SECTION + FAR + r, at_b(1))

    def far_kv(s, r):
        block = kv.at[s, (b + 3) % 4, r]
        return rc(block, block, s * SENDS + S_FK, s * PER_SECTION + FAR + r, at_b(1))

    def far_v(s, r):
        block = kv.at[s, (b + 1) % 4, r, 1]
        return rc(block, block, s * SENDS + S_FV, s * PER_SECTION + FAR + r, at_b(3))

    uses_l = (c == 0) | (b > 0)
    uses_r = (c == 0) | (b == 3)
    sends_r = (c == 0) | (b < 3)
    sends_l = (c == 0) | (b == 0)
    sends_v = (c == 1) & (b == 1)
    sends_far_k = (c == 0) | (b == 2)
    sends_far_kv = (c == 1) & (b == 1)
    sends_far_v = (c == 0) | (b == 0)

    def start_hops(s, r):
        @pl.when(sends_r)
        def _():
            hop_r(s, r).start()

        @pl.when(sends_l)
        def _():
            hop_l(s, r).start()

        @pl.when(sends_v)
        def _():
            hop_v(s, r).start()

    def take_left(s, r):
        @pl.when(uses_l)
        def _():
            hop_r(s, r).wait_recv()

        @pl.when(sends_far_k)
        def _():
            far_k(s, r).start()

        @pl.when(sends_far_kv)
        def _():
            far_kv(s, r).start()

    def take_right(s, r):
        @pl.when(uses_r)
        def _():
            hop_l(s, r).wait_recv()

        @pl.when((c == 1) & (b == 0))
        def _():
            hop_v(s, r).wait_recv()

        @pl.when(sends_far_v)
        def _():
            far_v(s, r).start()

    def take_far(s, r):
        @pl.when(uses_r)
        def _():
            all_of(kv.at[s, b, r], s * SENDS + S_FK, s * PER_SECTION + FAR + r).wait_recv()

        @pl.when((c == 1) & (b == 2))
        def _():
            far_kv(s, r).wait_recv()

    def section_start(s):
        normed = layer_norm(x_ref[...].astype(F32)).astype(BF16)

        def project(part, column, scale):
            made = silu(dot(normed, w_all[s, :, column : column + DIM])) * scale
            for h in range(4):
                snd[s, h, part] = made[:, h * HD : (h + 1) * HD].astype(BF16)

        project(0, 1536, 1.0)
        project(1, 512, 1.0)
        for d in (1, 3):
            kv_a(s, d).start()

        @pl.when(c == 0)
        def _():
            kv_a(s, 2).start()

        cp_kv = pltpu.make_async_copy(snd.at[s, a, pl.ds(0, 2)], kv.at[s, b, a], lsem.at[7])
        cp_kv.start()
        cp_kv.wait()

        start_hops(s, a)

        project(2, 1024, 0.5)
        cp_q = pltpu.make_async_copy(snd.at[s, a, 2], qs.at[s, a], lsem.at[8])
        cp_q.start()
        gates[...] = silu(dot(normed, w_all[s, :, 0:DIM])).astype(BF16)
        cp_q.wait()
        all_of(kv.at[s, b, pl.ds(0, 2)], s * SENDS + S_KV, 0).wait_send()
        for d in (1, 3, 2):
            q_a(s, d).start()

        @pl.when(c == 1)
        def _():
            kv_a(s, 2).start()

    def section_end(s):
        all_of(mix.at[s, pl.ds(0, 3)], s * SENDS + S_MIX, s * PER_SECTION + MIX).wait_recv()
        mixed = jnp.concatenate([mix[s, h] for h in range(4)], axis=1).astype(F32)
        gated = (layer_norm(mixed) * gates[...].astype(F32)).astype(BF16)
        return x_ref[...].astype(F32) + dot(gated, ow_all[s])

    def send_mix(s, r):
        @pl.when(r == a)
        def _():
            mix[s, a] = acc[r].astype(BF16)

        @pl.when(r != a)
        def _():
            mix_snd[s, r] = acc[r].astype(BF16)
            mix_a(s, (r + 4 - a) % 4).start()

    def attend(s, first, blocks):
        m = (4 - first) * TOK
        queries = jnp.concatenate(
            [qs[s, first:4].reshape(m, HD), q_ext[first:4].reshape(m, HD)], axis=1
        )
        total = None
        for bb, r, masked in blocks:
            keys = jnp.concatenate([kv[s, bb, r, 0], k_ext[bb, r]], axis=1)
            u = lax.dot_general(
                queries, keys, (((1,), (1,)), ((), ())), preferred_element_type=F32
            )
            weights = u + u * jnp.tanh(u)
            parts = []
            for k in range(masked):
                ahead = 256 * (sa * r + sb * bb) - 256 * (sa * (first + k) + sb * b)
                part = weights[k * TOK : (k + 1) * TOK]
                parts.append(jnp.where(diff_ref[...] >= ahead, part, 0.0))
            if masked:
                if first + masked < 4:
                    parts.append(weights[masked * TOK :])
                weights = jnp.concatenate(parts, axis=0)
            term = dot(weights.astype(BF16), kv[s, bb, r, 1])
            total = term if total is None else total + term
        acc[first:4] += total.reshape(4 - first, TOK, HD)

    def grad_partials():
        all_of(g_rcv.at[pl.ds(0, 3)], S_GRAD, GRAD).wait_recv()
        half_snd[...] = partial_half(1 - c).astype(BF16)
        half.start()
        half_own[...] = partial_half(c)

    def grad_stage_a():
        half.wait_recv()
        summed = half_own[...] + half_rcv[...].astype(F32)
        half_own[...] = summed
        for k in range(4):
            ga_snd[k] = summed[k * 128 : (k + 1) * 128].astype(BF16)
        for d in (2, 1, 3):
            ga[d - 1].start()

    def grad_stage_b():
        all_of(ga_rcv.at[pl.ds(0, 3)], S_GA, GA).wait_recv()
        total = half_own[pl.ds(pl.multiple_of(a * 128, 128), 128), :]
        for d in (1, 2, 3):
            total = total + ga_rcv[(a + d) % 4].astype(F32)
        half_own[0:128, :] = total
        for k in range(4):
            gb_snd[k] = total[k * 32 : (k + 1) * 32].astype(BF16)
        for d in (2, 1, 3):
            gb[d - 1].start()

    def section(s, carry):
        @pl.when(s == 1)
        def _():
            x_ref[...] = section_end(0).astype(BF16)

        section_start(s)
        acc[...] = jnp.zeros_like(acc)
        odd = a % 2
        pair = a // 2
        mate, next_row, last_row = a + 1 - 2 * odd, (a + 3 + 2 * odd) % 4, (a + 2) % 4
        for d in (3 - 2 * odd, 1 + 2 * odd):
            kv_a(s, d).wait_recv()

            @pl.when(c == 0)
            def _(d=d):
                start_hops(s, (a + 4 - d) % 4)

        @pl.when(c == 0)
        def _():
            kv_a(s, 2).wait_recv()
            start_hops(s, last_row)
            take_left(s, a)
            take_right(s, a)

        all_of(qs.at[s, pl.ds(0, 3)], s * SENDS + S_Q, s * PER_SECTION + Q_A).wait_recv()

        @pl.when(c == 1)
        def _():
            for r in (mate, next_row):
                start_hops(s, r)

        @pl.when(c == 1)
        def _():
            kv_a(s, 2).wait_recv()
            start_hops(s, last_row)

        takes = {
            0: ((0, mate),),
            1: ((0, next_row), (1, a)),
            2: ((1, mate),),
            3: ((0, last_row), (1, next_row)),
            4: ((1, last_row),),
        }
        for n, (kind, second) in enumerate(
            ((0, 0), (0, 1), (1, 0), (2, 0), (1, 1), (2, 1), (3, 0), (3, 1))
        ):
            p = 1 - pair if second else pair
            bb = (b + (0, 3, 1, 2)[kind]) % 4

            for core, r in takes.get(n, ()):

                @pl.when(c == core)
                def _(r=r):
                    take_left(s, r)
                    take_right(s, r)

            if n in (0, 2):

                @pl.when((s == 1) & (c == 1 - n // 2))
                def _():
                    grad_stage_a()

            if kind == 3:
                take_far(s, 2 * p)
                take_far(s, 2 * p + 1)

            split = (p >= 0) if kind == 0 else (c == 0)

            @pl.when(split & (p == 0))
            def _(bb=bb):
                attend(s, 0, ((bb, 0, 1), (bb, 1, 2)))

            @pl.when(split & (p == 1))
            def _(bb=bb):
                attend(s, 2, ((bb, 2, 1), (bb, 3, 2)))

            if kind:

                @pl.when((c == 1) & (bb < b))
                def _(bb=bb, p=p):
                    attend(s, 0, ((bb, 2 * p, 0), (bb, 2 * p + 1, 0)))

        for r in range(4):
            send_mix(s, r)

        @pl.when(s == 0)
        def _():
            grad_partials()

        return carry

    cp_go.wait()
    lax.fori_loop(0, 2, section, 0)
    grad_stage_b()
    states_ref[...] = (layer_norm(section_end(1)) * gain_ref[...]).astype(BF16)

    for s in (0, 1):
        kv_a(s, 2).wait_send()
        all_of(qs.at[s, pl.ds(0, 3)], s * SENDS + S_Q, 0).wait_send()
        all_of(mix.at[s, pl.ds(0, 3)], s * SENDS + S_MIX, 0).wait_send()
        whole, part = kv.at[s, b], kv.at[s, b, pl.ds(0, 2)]
        for used, ref, left in (
            (sends_r, whole, S_R), (sends_l, whole, S_L), (sends_v, part, S_L),
            (sends_far_k, part, S_FK), (sends_far_kv, whole, S_FK), (sends_far_v, part, S_FV),
        ):

            @pl.when(used)
            def _(ref=ref, left=left, s=s):
                all_of(ref, s * SENDS + left, 0).wait_send()

    all_of(gb_rcv.at[pl.ds(0, 3)], S_GB, GB).wait_recv()
    total = half_own[pl.ds(pl.multiple_of(b * 32, 32), 32), :]
    for d in (1, 2, 3):
        total = total + gb_rcv[(b + d) % 4].astype(F32)
    tg_ref[...] = total
    for ref, left in (
        (req_rcv, S_REQ), (rows_rcv, S_ROWS), (g_rcv, S_GRAD), (ga_rcv, S_GA), (gb_rcv, S_GB),
    ):
        all_of(ref.at[pl.ds(0, 3)], left, 0).wait_send()
    for cp in (wgt, owgt, half):
        cp.wait_send()


def body(
    item_table, item_owner, item_slot, seq_lengths, row_grads, proj_weight, out_weight, final_gain
):
    vmem = pl.BlockSpec(memory_space=pltpu.VMEM)
    hbm = pl.BlockSpec(memory_space=pl.ANY)

    def buf(*shape, dtype=BF16):
        return pltpu.VMEM(shape, dtype)

    states, table_grad = pl.pallas_call(
        kernel,
        out_shape=(
            jax.ShapeDtypeStruct((TOK, DIM), BF16),
            jax.ShapeDtypeStruct((32, DIM), F32),
        ),
        in_specs=[hbm] * 8,
        out_specs=(vmem, vmem),
        scratch_shapes=[
            buf(1, TOK, dtype=jnp.int32), buf(1, TOK, dtype=jnp.int32),
            pltpu.SMEM((2, 2), jnp.int32), buf(1, DIM, dtype=F32),
            buf(OWNED, DIM), buf(TOK, DIM), buf(2, DIM, 4 * DIM), buf(2, DIM, DIM),
            buf(4, 8, CAP, dtype=F32), buf(4, 8, CAP, dtype=F32),
            buf(4, CAP, DIM), buf(4, CAP, DIM), buf(4, CAP, DIM), buf(4, CAP, DIM),
            buf(TOK, DIM), buf(2, 4, 3, TOK, HD), buf(TOK, DIM),
            buf(2, 4, 4, 2, TOK, HD), buf(2, 4, TOK, HD), buf(4, TOK, HD, dtype=F32),
            buf(2, 4, TOK, HD), buf(2, 4, TOK, HD),
            buf(512, DIM), buf(512, DIM, dtype=F32), buf(512, DIM),
            buf(4, 128, DIM), buf(4, 128, DIM), buf(4, 32, DIM), buf(4, 32, DIM),
            buf(4, TOK, HD), buf(4, 4, TOK, HD), buf(TOK, TOK, dtype=jnp.int32),
            pltpu.SemaphoreType.DMA((N_SEND,)),
            pltpu.SemaphoreType.DMA((N_RECV,)),
            pltpu.SemaphoreType.DMA((10,)),
        ],
        compiler_params=pltpu.CompilerParams(
            collective_id=0, has_side_effects=True, vmem_limit_bytes=56 << 20
        ),
    )(
        item_owner.reshape(1, TOK),
        item_slot.reshape(1, TOK),
        seq_lengths.reshape(2, 2),
        final_gain.reshape(1, DIM),
        item_table,
        row_grads.reshape(TOK, DIM),
        proj_weight.reshape(DIM, 4 * DIM),
        out_weight.reshape(DIM, DIM),
    )
    def hand_out(states_in, grad_in, states_out, grad_out):
        states_out[...] = states_in[...]
        grad_out[...] = grad_in[...]

    states, table_grad = pl.pallas_call(
        hand_out,
        out_shape=(
            jax.ShapeDtypeStruct((TOK, DIM), BF16),
            jax.ShapeDtypeStruct((32, DIM), F32),
        ),
        in_specs=[vmem, vmem],
        out_specs=(vmem, vmem),
    )(states, table_grad)
    return states.reshape(1, 1, TOK, DIM), table_grad


def solution(mesh):
    placed = (
        P("emb", None),
        P("emb", "phase", "row", None),
        P("emb", "phase", "row"),
        P("emb", None, None),
        P("emb", "phase", "row", None),
        P("phase", None, None),
        P("phase", None, None),
        P(),
    )
    return jax.shard_map(
        body,
        mesh=mesh,
        in_specs=placed,
        out_specs=(P("emb", "phase", "row", None), P(("emb", "row", "phase"), None)),
        check_vma=False,
    )
```

```python
import functools

import jax
import jax.numpy as jnp
from jax import lax
from jax.experimental import pallas as pl
from jax.experimental.pallas import tpu as pltpu
from jax.sharding import PartitionSpec as P

MESH = pl.DeviceIdType.MESH
F32 = jnp.float32
BF16 = jnp.bfloat16
EPS = 1e-05
BIG = 2.0**40

TOK = 256
DIM = 512
HD = 128
CAP = 128
OWNED = 1024

KV_A, Q_A, HOP_R, HOP_L, FAR, MIX = 0, 3, 4, 8, 12, 16
PER_SECTION = 17
REQ, ROWS, GRAD, WGT, OWGT, HALF, GA, GB = 34, 37, 38, 39, 40, 41, 42, 43
N_RECV = 44
S_KV, _, S_Q, S_R, S_L, S_FK, S_FV, S_MIX = range(8)
SENDS = 8
S_REQ, S_ROWS, S_GRAD, S_WGT, S_OWGT, S_HALF, S_GA, S_GB = range(16, 24)
N_SEND = 24


def dot(left, right):
    return jnp.dot(left, right, preferred_element_type=F32)


def layer_norm(values):
    average = jnp.mean(values, axis=-1, keepdims=True)
    centered = values - average
    return centered * lax.rsqrt(jnp.mean(centered * centered, axis=-1, keepdims=True) + EPS)


def silu(v):
    u = 0.5 * v
    return u + u * jnp.tanh(u)


def iota(shape, dim):
    return lax.broadcasted_iota(jnp.int32, shape, dim)


def kernel(
    owner_hbm, slot_hbm, len_hbm, gain_hbm, table_hbm, grads_hbm, w_hbm, ow_hbm,
    states_ref, tg_ref,
    owner_ref, slot_ref, len_ref, gain_ref, table, grads, w_all, ow_all, req_snd, req_rcv, rows_snd, rows_rcv, go_snd, g_rcv,
    x_ref, snd, gates, kv, qs, acc, mix_snd, mix, half_snd, half_own, half_rcv,
    ga_snd, ga_rcv, gb_snd, gb_rcv, q_ext, k_ext, diff_ref, ssem, rsem, lsem,
):
    ex = lax.axis_index("emb")
    row = lax.axis_index("row")
    c = lax.axis_index("phase")
    z, y = row // 4, row % 4
    a = z * (1 - c) + y * c
    b = y * (1 - c) + z * c
    sa, sb = 4 - 3 * c, 1 + 3 * c

    def at_a(d):
        return {"row": sa * ((a + d) % 4) + sb * b}

    def at_b(d):
        return {"row": sa * a + sb * ((b + d) % 4)}

    def at_x(d):
        return {"emb": (ex + d) % 4}

    other = {"phase": 1 - c}

    def rc(src, dst, left, came, dev):
        return pltpu.make_async_remote_copy(
            src_ref=src, dst_ref=dst, send_sem=ssem.at[left], recv_sem=rsem.at[came],
            device_id=dev, device_id_type=MESH,
        )

    def all_of(ref, left, came):
        return rc(ref, ref, left, came, other)

    barrier = pltpu.get_barrier_semaphore()
    for d in (1, 2, 3):
        for dev in (at_x(d), at_a(d), at_b(d)):
            pl.semaphore_signal(barrier, inc=1, device_id=dev, device_id_type=MESH)
    pl.semaphore_signal(barrier, inc=1, device_id=other, device_id_type=MESH)
    small = [
        pltpu.make_async_copy(src, dst, lsem.at[4 + k])
        for k, (src, dst) in enumerate(
            (
                (owner_hbm, owner_ref), (slot_hbm, slot_ref), (len_hbm, len_ref),
                (gain_hbm, gain_ref),
            )
        )
    ]
    for cp in small:
        cp.start()
    cp_table = pltpu.make_async_copy(table_hbm, table, lsem.at[0])
    cp_grads = pltpu.make_async_copy(grads_hbm, grads, lsem.at[1])
    cp_w = pltpu.make_async_copy(w_hbm, w_all.at[c], lsem.at[2])
    cp_ow = pltpu.make_async_copy(ow_hbm, ow_all.at[c], lsem.at[3])
    for cp in (cp_table, cp_grads, cp_w, cp_ow):
        cp.start()
    for cp in small:
        cp.wait()

    own_row = owner_ref[...].astype(F32)
    slot_row = slot_ref[...].astype(F32)
    ti, tj = iota((TOK, TOK), 0), iota((TOK, TOK), 1)
    eye = ti == tj
    own_col = jnp.sum(jnp.where(eye, own_row, 0.0), axis=1, keepdims=True)
    slot_col = jnp.sum(jnp.where(eye, slot_row, 0.0), axis=1, keepdims=True)
    same = own_col == own_row
    rank_col = jnp.sum(jnp.where(same & (tj < ti), 1.0, 0.0), axis=1, keepdims=True)
    rank_row = jnp.sum(jnp.where(same & (ti < tj), 1.0, 0.0), axis=0, keepdims=True)
    key_col = (own_col * CAP + rank_col).astype(jnp.int32)
    key_row = (own_row * CAP + rank_row).astype(jnp.int32)
    place = key_col == iota((TOK, 4 * CAP), 1)
    req_row = jnp.sum(jnp.where(place, slot_col + 1.0, 0.0), axis=0, keepdims=True) - 1.0
    for e in range(4):
        req_snd[e] = jnp.broadcast_to(req_row[:, e * CAP : (e + 1) * CAP], (8, CAP))
    cp_req = pltpu.make_async_copy(req_snd.at[ex], req_rcv.at[ex], lsem.at[4])
    cp_req.start()
    bound = len_ref[c, 0]
    lane0 = iota((TOK, HD), 1) == 0
    pos = iota((TOK, HD), 0)
    diff_ref[...] = ti - tj
    for k in range(4):
        after = (pos + 256 * (sa * k + sb * b) >= bound) & lane0
        q_ext[k] = jnp.where(after, -BIG, 0.0).astype(BF16)
        for h in range(4):
            before = (pos + 256 * (sa * k + sb * h) < bound) & lane0
            k_ext[h, k] = jnp.where(before, 1.0, 0.0).astype(BF16)
    pl.semaphore_wait(barrier, 10)
    req = [rc(req_snd.at[(ex + d) % 4], req_rcv.at[ex], S_REQ, REQ + d - 1, at_x(d)) for d in (1, 2, 3)]
    for d in (2, 1, 3):
        req[d - 1].start()
    wgt = rc(w_hbm, w_all.at[c], S_WGT, WGT, other)
    owgt = rc(ow_hbm, ow_all.at[c], S_OWGT, OWGT, other)
    wgt.start()
    owgt.start()

    cp_grads.wait()
    place_t = (key_row == iota((4 * CAP, TOK), 0)).astype(F32).astype(BF16)
    for e in range(4):
        go_snd[e] = dot(place_t[e * CAP : (e + 1) * CAP], grads[...]).astype(BF16)
    cp_go = pltpu.make_async_copy(go_snd.at[ex], g_rcv.at[ex], lsem.at[5])
    cp_go.start()

    cp_req.wait()
    cp_table.wait()
    eye_cap = iota((CAP, CAP), 0) == iota((CAP, CAP), 1)

    def look_up(q):
        wanted = jnp.sum(
            jnp.where(eye_cap, req_rcv[q][0:1], 0.0), axis=1, keepdims=True
        ).astype(jnp.int32)
        picked = (wanted == iota((CAP, OWNED), 1)).astype(F32).astype(BF16)
        rows_snd[q] = dot(picked, table[...]).astype(BF16)

    rows = [rc(rows_snd.at[(ex + d) % 4], rows_rcv.at[ex], S_ROWS, ROWS, at_x(d)) for d in (1, 2, 3)]
    look_up(ex)
    cp_rows = pltpu.make_async_copy(rows_snd.at[ex], rows_rcv.at[ex], lsem.at[6])
    cp_rows.start()
    for d in (1, 3, 2):
        req[d - 1].wait_recv()
        look_up((ex + 4 - d) % 4)
        rows[3 - d].start()
    cp_rows.wait()
    all_of(rows_rcv.at[pl.ds(0, 3)], S_ROWS, ROWS).wait_recv()
    embedded = dot(
        place.astype(F32).astype(BF16), rows_rcv[...].reshape(4 * CAP, DIM)
    )
    x_ref[...] = embedded.astype(BF16)

    grad = [rc(go_snd.at[(ex + d) % 4], g_rcv.at[ex], S_GRAD, GRAD, at_x(d)) for d in (1, 2, 3)]
    for d in (2, 1, 3):
        grad[d - 1].start()
    cp_w.wait()
    cp_ow.wait()
    wgt.wait_recv()
    owgt.wait_recv()

    def partial_half(cc):
        j = iota((512, 1), 0)
        aj, bj, i = j // 128, (j // 32) % 4, j % 32
        slot = ((4 - 3 * cc) * aj + (1 + 3 * cc) * bj) * 64 + cc * 32 + i
        total = None
        for q in range(4):
            hit = (slot == req_rcv[q][0:1].astype(jnp.int32)).astype(F32).astype(BF16)
            term = dot(hit, g_rcv[q])
            total = term if total is None else total + term
        return total

    half = rc(half_snd, half_rcv, S_HALF, HALF, other)
    ga = [rc(ga_snd.at[(a + d) % 4], ga_rcv.at[a], S_GA, GA, at_a(d)) for d in (1, 2, 3)]
    gb = [rc(gb_snd.at[(b + d) % 4], gb_rcv.at[b], S_GB, GB, at_b(d)) for d in (1, 2, 3)]

    def kv_a(s, d):
        return rc(snd.at[s, (a + d) % 4, pl.ds(0, 2)], kv.at[s, b, a], s * SENDS + S_KV + 1 - d % 2, s * PER_SECTION + KV_A + d - 1, at_a(d))

    def q_a(s, d):
        return rc(snd.at[s, (a + d) % 4, 2], qs.at[s, a], s * SENDS + S_Q, s * PER_SECTION + Q_A, at_a(d))

    def mix_a(s, d):
        return rc(mix_snd.at[s, (a + d) % 4], mix.at[s, a], s * SENDS + S_MIX, s * PER_SECTION + MIX, at_a(d))

    def hop_r(s, r):
        block = kv.at[s, b, r]
        return rc(block, block, s * SENDS + S_R, s * PER_SECTION + HOP_R + r, at_b(1))

    def hop_l(s, r):
        block = kv.at[s, b, r]
        return rc(block, block, s * SENDS + S_L, s * PER_SECTION + HOP_L + r, at_b(3))

    def hop_v(s, r):
        block = kv.at[s, b, r, 1]
        return rc(block, block, s * SENDS + S_L, s * PER_SECTION + HOP_L + r, at_b(3))

    def far_k(s, r):
        block = kv.at[s, (b + 3) % 4, r, 0]
        return rc(block, block, s * SENDS + S_FK, s * PER_SECTION + FAR + r, at_b(1))

    def far_kv(s, r):
        block = kv.at[s, (b + 3) % 4, r]
        return rc(block, block, s * SENDS + S_FK, s * PER_SECTION + FAR + r, at_b(1))

    def far_v(s, r):
        block = kv.at[s, (b + 1) % 4, r, 1]
        return rc(block, block, s * SENDS + S_FV, s * PER_SECTION + FAR + r, at_b(3))

    uses_l = (c == 0) | (b > 0)
    uses_r = (c == 0) | (b == 3)
    sends_r = (c == 0) | (b < 3)
    sends_l = (c == 0) | (b == 0)
    sends_v = (c == 1) & (b == 1)
    sends_far_k = (c == 0) | (b == 2)
    sends_far_kv = (c == 1) & (b == 1)
    sends_far_v = (c == 0) | (b == 0)

    def start_hops(s, r):
        @pl.when(sends_r)
        def _():
            hop_r(s, r).start()

        @pl.when(sends_l)
        def _():
            hop_l(s, r).start()

        @pl.when(sends_v)
        def _():
            hop_v(s, r).start()

    def take_left(s, r):
        @pl.when(uses_l)
        def _():
            hop_r(s, r).wait_recv()

        @pl.when(sends_far_k)
        def _():
            far_k(s, r).start()

        @pl.when(sends_far_kv)
        def _():
            far_kv(s, r).start()

    def take_right(s, r):
        @pl.when(uses_r)
        def _():
            hop_l(s, r).wait_recv()

        @pl.when((c == 1) & (b == 0))
        def _():
            hop_v(s, r).wait_recv()

        @pl.when(sends_far_v)
        def _():
            far_v(s, r).start()

    def take_far(s, r):
        @pl.when(uses_r)
        def _():
            all_of(kv.at[s, b, r], s * SENDS + S_FK, s * PER_SECTION + FAR + r).wait_recv()

        @pl.when((c == 1) & (b == 2))
        def _():
            far_kv(s, r).wait_recv()

    def section_start(s):
        normed = layer_norm(x_ref[...].astype(F32)).astype(BF16)

        def project(part, column, scale):
            made = silu(dot(normed, w_all[s, :, column : column + DIM])) * scale
            for h in range(4):
                snd[s, h, part] = made[:, h * HD : (h + 1) * HD].astype(BF16)

        project(0, 1536, 1.0)
        project(1, 512, 1.0)
        for d in (1, 3):
            kv_a(s, d).start()

        @pl.when(c == 0)
        def _():
            kv_a(s, 2).start()

        cp_kv = pltpu.make_async_copy(snd.at[s, a, pl.ds(0, 2)], kv.at[s, b, a], lsem.at[7])
        cp_kv.start()
        cp_kv.wait()

        start_hops(s, a)

        project(2, 1024, 0.5)
        cp_q = pltpu.make_async_copy(snd.at[s, a, 2], qs.at[s, a], lsem.at[8])
        cp_q.start()
        gates[...] = silu(dot(normed, w_all[s, :, 0:DIM])).astype(BF16)
        cp_q.wait()
        all_of(kv.at[s, b, pl.ds(0, 2)], s * SENDS + S_KV, 0).wait_send()
        for d in (1, 3, 2):
            q_a(s, d).start()

        @pl.when(c == 1)
        def _():
            kv_a(s, 2).start()

    def section_end(s):
        all_of(mix.at[s, pl.ds(0, 3)], s * SENDS + S_MIX, s * PER_SECTION + MIX).wait_recv()
        mixed = jnp.concatenate([mix[s, h] for h in range(4)], axis=1).astype(F32)
        gated = (layer_norm(mixed) * gates[...].astype(F32)).astype(BF16)
        return x_ref[...].astype(F32) + dot(gated, ow_all[s])

    def send_mix(s, r):
        @pl.when(r == a)
        def _():
            mix[s, a] = acc[r].astype(BF16)

        @pl.when(r != a)
        def _():
            mix_snd[s, r] = acc[r].astype(BF16)
            mix_a(s, (r + 4 - a) % 4).start()

    def attend(s, first, blocks):
        m = (4 - first) * TOK
        queries = jnp.concatenate(
            [qs[s, first:4].reshape(m, HD), q_ext[first:4].reshape(m, HD)], axis=1
        )
        total = None
        for bb, r, masked in blocks:
            keys = jnp.concatenate([kv[s, bb, r, 0], k_ext[bb, r]], axis=1)
            u = lax.dot_general(
                queries, keys, (((1,), (1,)), ((), ())), preferred_element_type=F32
            )
            weights = u + u * jnp.tanh(u)
            parts = []
            for k in range(masked):
                ahead = 256 * (sa * r + sb * bb) - 256 * (sa * (first + k) + sb * b)
                part = weights[k * TOK : (k + 1) * TOK]
                parts.append(jnp.where(diff_ref[...] >= ahead, part, 0.0))
            if masked:
                if first + masked < 4:
                    parts.append(weights[masked * TOK :])
                weights = jnp.concatenate(parts, axis=0)
            term = dot(weights.astype(BF16), kv[s, bb, r, 1])
            total = term if total is None else total + term
        acc[first:4] += total.reshape(4 - first, TOK, HD)

    def grad_partials():
        all_of(g_rcv.at[pl.ds(0, 3)], S_GRAD, GRAD).wait_recv()
        half_snd[...] = partial_half(1 - c).astype(BF16)
        half.start()
        half_own[...] = partial_half(c)

    def grad_stage_a():
        half.wait_recv()
        summed = half_own[...] + half_rcv[...].astype(F32)
        half_own[...] = summed
        for k in range(4):
            ga_snd[k] = summed[k * 128 : (k + 1) * 128].astype(BF16)
        for d in (2, 1, 3):
            ga[d - 1].start()

    def grad_stage_b():
        all_of(ga_rcv.at[pl.ds(0, 3)], S_GA, GA).wait_recv()
        total = half_own[pl.ds(pl.multiple_of(a * 128, 128), 128), :]
        for d in (1, 2, 3):
            total = total + ga_rcv[(a + d) % 4].astype(F32)
        half_own[0:128, :] = total
        for k in range(4):
            gb_snd[k] = total[k * 32 : (k + 1) * 32].astype(BF16)
        for d in (2, 1, 3):
            gb[d - 1].start()

    def section(s, carry):
        @pl.when(s == 1)
        def _():
            x_ref[...] = section_end(0).astype(BF16)

        section_start(s)
        acc[...] = jnp.zeros_like(acc)
        odd = a % 2
        pair = a // 2
        mate, next_row, last_row = a + 1 - 2 * odd, (a + 3 + 2 * odd) % 4, (a + 2) % 4
        for d in (3 - 2 * odd, 1 + 2 * odd):
            kv_a(s, d).wait_recv()

            @pl.when(c == 0)
            def _(d=d):
                start_hops(s, (a + 4 - d) % 4)

        @pl.when(c == 0)
        def _():
            kv_a(s, 2).wait_recv()
            start_hops(s, last_row)
            take_left(s, a)
            take_right(s, a)

        all_of(qs.at[s, pl.ds(0, 3)], s * SENDS + S_Q, s * PER_SECTION + Q_A).wait_recv()

        @pl.when(c == 1)
        def _():
            for r in (mate, next_row):
                start_hops(s, r)

        @pl.when(c == 1)
        def _():
            kv_a(s, 2).wait_recv()
            start_hops(s, last_row)

        takes = {
            0: ((0, mate),),
            1: ((0, next_row), (1, a)),
            2: ((0, last_row), (1, mate)),
            3: ((1, next_row),),
            4: ((1, last_row),),
        }
        for n, (kind, second) in enumerate(
            ((0, 0), (0, 1), (1, 0), (2, 0), (1, 1), (2, 1), (3, 0), (3, 1))
        ):
            p = 1 - pair if second else pair
            bb = (b + (0, 3, 1, 2)[kind]) % 4

            for core, r in takes.get(n, ()):

                @pl.when(c == core)
                def _(r=r):
                    take_left(s, r)
                    take_right(s, r)

            if n in (0, 2):

                @pl.when((s == 1) & (c == 1 - n // 2))
                def _():
                    grad_stage_a()

            if kind == 3:
                take_far(s, 2 * p)
                take_far(s, 2 * p + 1)

            split = (p >= 0) if kind == 0 else (c == 0)

            @pl.when(split & (p == 0))
            def _(bb=bb):
                attend(s, 0, ((bb, 0, 1), (bb, 1, 2)))

            @pl.when(split & (p == 1))
            def _(bb=bb):
                attend(s, 2, ((bb, 2, 1), (bb, 3, 2)))

            if kind:

                @pl.when((c == 1) & (bb < b))
                def _(bb=bb, p=p):
                    attend(s, 0, ((bb, 2 * p, 0), (bb, 2 * p + 1, 0)))

        for r in range(4):
            send_mix(s, r)

        @pl.when(s == 0)
        def _():
            grad_partials()

        return carry

    cp_go.wait()
    lax.fori_loop(0, 2, section, 0)
    grad_stage_b()
    states_ref[...] = (layer_norm(section_end(1)) * gain_ref[...]).astype(BF16)

    for s in (0, 1):
        kv_a(s, 2).wait_send()
        all_of(qs.at[s, pl.ds(0, 3)], s * SENDS + S_Q, 0).wait_send()
        all_of(mix.at[s, pl.ds(0, 3)], s * SENDS + S_MIX, 0).wait_send()
        whole, part = kv.at[s, b], kv.at[s, b, pl.ds(0, 2)]
        for used, ref, left in (
            (sends_r, whole, S_R), (sends_l, whole, S_L), (sends_v, part, S_L),
            (sends_far_k, part, S_FK), (sends_far_kv, whole, S_FK), (sends_far_v, part, S_FV),
        ):

            @pl.when(used)
            def _(ref=ref, left=left, s=s):
                all_of(ref, s * SENDS + left, 0).wait_send()

    all_of(gb_rcv.at[pl.ds(0, 3)], S_GB, GB).wait_recv()
    total = half_own[pl.ds(pl.multiple_of(b * 32, 32), 32), :]
    for d in (1, 2, 3):
        total = total + gb_rcv[(b + d) % 4].astype(F32)
    tg_ref[...] = total
    for ref, left in (
        (req_rcv, S_REQ), (rows_rcv, S_ROWS), (g_rcv, S_GRAD), (ga_rcv, S_GA), (gb_rcv, S_GB),
    ):
        all_of(ref.at[pl.ds(0, 3)], left, 0).wait_send()
    for cp in (wgt, owgt, half):
        cp.wait_send()


def body(
    item_table, item_owner, item_slot, seq_lengths, row_grads, proj_weight, out_weight, final_gain
):
    vmem = pl.BlockSpec(memory_space=pltpu.VMEM)
    hbm = pl.BlockSpec(memory_space=pl.ANY)

    def buf(*shape, dtype=BF16):
        return pltpu.VMEM(shape, dtype)

    states, table_grad = pl.pallas_call(
        kernel,
        out_shape=(
            jax.ShapeDtypeStruct((TOK, DIM), BF16),
            jax.ShapeDtypeStruct((32, DIM), F32),
        ),
        in_specs=[hbm] * 8,
        out_specs=(vmem, vmem),
        scratch_shapes=[
            buf(1, TOK, dtype=jnp.int32), buf(1, TOK, dtype=jnp.int32),
            pltpu.SMEM((2, 2), jnp.int32), buf(1, DIM, dtype=F32),
            buf(OWNED, DIM), buf(TOK, DIM), buf(2, DIM, 4 * DIM), buf(2, DIM, DIM),
            buf(4, 8, CAP, dtype=F32), buf(4, 8, CAP, dtype=F32),
            buf(4, CAP, DIM), buf(4, CAP, DIM), buf(4, CAP, DIM), buf(4, CAP, DIM),
            buf(TOK, DIM), buf(2, 4, 3, TOK, HD), buf(TOK, DIM),
            buf(2, 4, 4, 2, TOK, HD), buf(2, 4, TOK, HD), buf(4, TOK, HD, dtype=F32),
            buf(2, 4, TOK, HD), buf(2, 4, TOK, HD),
            buf(512, DIM), buf(512, DIM, dtype=F32), buf(512, DIM),
            buf(4, 128, DIM), buf(4, 128, DIM), buf(4, 32, DIM), buf(4, 32, DIM),
            buf(4, TOK, HD), buf(4, 4, TOK, HD), buf(TOK, TOK, dtype=jnp.int32),
            pltpu.SemaphoreType.DMA((N_SEND,)),
            pltpu.SemaphoreType.DMA((N_RECV,)),
            pltpu.SemaphoreType.DMA((10,)),
        ],
        compiler_params=pltpu.CompilerParams(
            collective_id=0, has_side_effects=True, vmem_limit_bytes=56 << 20
        ),
    )(
        item_owner.reshape(1, TOK),
        item_slot.reshape(1, TOK),
        seq_lengths.reshape(2, 2),
        final_gain.reshape(1, DIM),
        item_table,
        row_grads.reshape(TOK, DIM),
        proj_weight.reshape(DIM, 4 * DIM),
        out_weight.reshape(DIM, DIM),
    )
    def hand_out(states_in, grad_in, states_out, grad_out):
        states_out[...] = states_in[...]
        grad_out[...] = grad_in[...]

    states, table_grad = pl.pallas_call(
        hand_out,
        out_shape=(
            jax.ShapeDtypeStruct((TOK, DIM), BF16),
            jax.ShapeDtypeStruct((32, DIM), F32),
        ),
        in_specs=[vmem, vmem],
        out_specs=(vmem, vmem),
    )(states, table_grad)
    return states.reshape(1, 1, TOK, DIM), table_grad


def solution(mesh):
    placed = (
        P("emb", None),
        P("emb", "phase", "row", None),
        P("emb", "phase", "row"),
        P("emb", None, None),
        P("emb", "phase", "row", None),
        P("phase", None, None),
        P("phase", None, None),
        P(),
    )
    return jax.shard_map(
        body,
        mesh=mesh,
        in_specs=placed,
        out_specs=(P("emb", "phase", "row", None), P(("emb", "row", "phase"), None)),
        check_vma=False,
    )
```
